32 devices in a mesh: dp: 16 (over z, y, core), section: 2 (over x).
Axes of the slice: x: 2, y: 2, z: 4, core: 2. Of those that a mesh axis runs over, the one named last changes fastest.
Arguments:
- patches: bfloat16 [48, 196, 768], P('dp'), may hold values from -6 to 6
- block_mask: int32 [48, 196], P('dp'), may hold values 0 or 1
- mask_token: bfloat16 [768], replicated, may hold values from -6 to 6
- norm_gains: float32 [2, 2, 768], P('section'), may hold values from 0.1 to 1.9
- norm_shifts: float32 [2, 2, 768], P('section'), may hold values from -2 to 2
- w_qkv: bfloat16 [2, 768, 2304], P('section'), may hold values from -0.21875 to 0.21875
- qv_bias: float32 [2, 2, 768], P('section'), may hold values from -3 to 3
- w_out: bfloat16 [2, 768, 768], P('section'), may hold values from -0.875 to 0.875
- out_bias: float32 [2, 768], P('section'), may hold values from -3 to 3
- w_up: bfloat16 [2, 768, 3072], P('section'), may hold values from -0.21875 to 0.21875
- up_bias: float32 [2, 3072], P('section'), may hold values from -3 to 3
- w_down: bfloat16 [2, 3072, 768], P('section'), may hold values from -0.15625 to 0.15625
- down_bias: float32 [2, 768], P('section'), may hold values from -3 to 3
- cotangent: bfloat16 [48, 196, 768], P('dp'), may hold values from -6 to 6
Outputs:
- boundary: float32 [2, 48, 196, 768], P('section', 'dp')
- token_grad: float32 [768], replicated
- gains_grad: float32 [2, 2, 768], P('section', None, 'dp')
- shifts_grad: float32 [2, 2, 768], P('section', None, 'dp')
- qkv_grad: float32 [2, 768, 2304], P('section', None, 'dp')
- qv_bias_grad: float32 [2, 2, 768], P('section', None, 'dp')
- out_grad: float32 [2, 768, 768], P('section', None, 'dp')
- out_bias_grad: float32 [2, 768], P('section', 'dp')
- up_grad: float32 [2, 768, 3072], P('section', None, 'dp')
- up_bias_grad: float32 [2, 3072], P('section', 'dp')
- down_grad: float32 [2, 3072, 768], P('section', None, 'dp')
- down_bias_grad: float32 [2, 768], P('section', 'dp')
The draws below stay inside these ranges and needn't reach their ends.
All inputs are finite; a program needn't handle non-finite values. No bound on the sum of `block_mask` on one device may be relied on, other than what follows from the above.
Results may differ from the reference program's by a relative error of at most 0.015.
Values may be sent and summed in bfloat16 or wider, within the bound.
A program may use at most 256 MiB of HBM per device.

```python
import math
import jax
import jax.numpy as jnp
from jax import lax

D = 768
HEADS = 12
FF = 3072
SEQ = 196
IMG_DEV = 3
IMAGES = 48


def with_ends(values, rng, least, top_value):
    index_at = [jax.random.randint(jax.random.fold_in(rng, axis), (), 0, length) for axis, length in enumerate(values.shape)]
    widest = values.shape.index(max(values.shape))
    next_to = index_at[:widest] + [(index_at[widest] + 1) % values.shape[widest]] + index_at[widest + 1:]
    return values.at[tuple(index_at)].set(least).at[tuple(next_to)].set(top_value)


def strengthened(values, rng, source, target, parts, factor):
    owner, partner = [(jnp.arange(values.shape[axis_at]) // (values.shape[axis_at] // parts)).reshape([-1 if axis == axis_at else 1 for axis in range(values.ndim)]) for axis_at in (source, target)]
    chosen = jax.random.permutation(rng, parts)[partner]
    strong = (owner == chosen) | (owner == (partner + parts // 2) % parts)
    return jnp.where(strong, factor * values, values)


def level_of(key, dims, cuts, least, top_value):
    factor_of = 1.0
    for position, shards_of in cuts:
        draws = jax.random.uniform(jax.random.fold_in(jax.random.fold_in(key, 6), position), (shards_of,), jnp.float32, least / len(cuts), top_value / len(cuts))
        factor_of = factor_of * jnp.repeat(jnp.exp(draws), dims[position] // shards_of).reshape((-1,) + (1,) * (len(dims) - 1 - position))
    return factor_of


def normal_values(key, extent, scale, most, cuts=(), dtype=jnp.bfloat16):
    level = level_of(key, extent, cuts, -0.22, 0.18) if cuts else 1.0
    drawn = jax.random.normal(key, extent, jnp.float32) * scale * level
    return jnp.minimum(jnp.maximum(drawn, -most), most).astype(dtype)


def bell_draw_with(rng, dims, scale, limit, pieces, heavy, dtype=jnp.bfloat16):
    values = scale * jax.random.normal(rng, dims, jnp.float32)
    if pieces:
        values = values * level_of(rng, dims, pieces, -0.22, 0.18)
    return jnp.clip(strengthened(values, jax.random.fold_in(rng, 3), *heavy), -limit, limit).astype(dtype)


def setup_inputs(seed: int = 0) -> dict:
    seeds = jax.random.split(jax.random.key(seed), 15)
    patches = normal_values(seeds[0], (IMAGES, SEQ, D), 1.0, 6.0, ((0, 16),))
    block_mask = with_ends((jax.random.randint(seeds[1], (IMAGES, SEQ), 0, 5) < 2).astype(jnp.int32), jax.random.fold_in(seeds[1], 1), 0, 1)
    mask_token = normal_values(seeds[2], (D,), 1.0, 6.0)
    norm_gains = jnp.clip(1.0 + 0.18 * jax.random.normal(seeds[3], (2, 2, D), jnp.float32), 0.1, 1.9)
    norm_shifts = normal_values(seeds[4], (2, 2, D), 0.3, 2.0, ((0, 2),), jnp.float32)
    w_qkv = normal_values(seeds[5], (2, D, 3 * D), D ** -0.5, 0.21875, ((0, 2),))
    qv_bias = normal_values(seeds[6], (2, 2, D), 0.5, 3.0, ((0, 2),), jnp.float32)
    w_out = normal_values(seeds[7], (2, D, D), (D // 16) ** -0.5, 0.875, ((0, 2),))
    out_bias = normal_values(seeds[8], (2, D), 0.5, 3.0, ((0, 2),), jnp.float32)
    w_up = normal_values(seeds[9], (2, D, FF), D ** -0.5, 0.21875, ((0, 2),))
    up_bias = normal_values(seeds[10], (2, FF), 0.5, 3.0, ((0, 2),), jnp.float32)
    w_down = normal_values(seeds[11], (2, FF, D), (FF // 2) ** -0.5, 0.15625, ((0, 2),))
    down_bias = normal_values(seeds[12], (2, D), 0.5, 3.0, ((0, 2),), jnp.float32)
    cotangent = bell_draw_with(seeds[13], (IMAGES, SEQ, D), 1.0, 6.0, ((0, 16),), (0, 2, 16, 2.0))
    return {"patches": patches, "block_mask": block_mask, "mask_token": mask_token, "norm_gains": norm_gains, "norm_shifts": norm_shifts, "w_qkv": w_qkv, "qv_bias": qv_bias, "w_out": w_out, "out_bias": out_bias, "w_up": w_up, "up_bias": up_bias, "w_down": w_down, "down_bias": down_bias, "cotangent": cotangent}


EPS = 1e-06
HIGH = lax.Precision.HIGHEST

@jax.custom_vjp
def low(v):
    return lax.optimization_barrier(v.astype(jnp.bfloat16)).astype(jnp.float32)

@jax.custom_vjp
def low_back(v):
    return v

def low_keep(v):
    return (low(v), None)

def low_pass(kept, grad):
    return (grad,)

def back_keep(v):
    return (v, None)

def back_low(kept, grad):
    return (low(grad),)
low.defvjp(low_keep, low_pass)
low_back.defvjp(back_keep, back_low)

def normalize(values, gain, shift):
    centered = values - lax.optimization_barrier(jnp.mean(values, axis=-1, keepdims=True))
    variance = lax.optimization_barrier(jnp.mean(centered * centered, axis=-1, keepdims=True))
    return centered * lax.rsqrt(variance + EPS) * gain + shift

def project(left, right):
    return jnp.einsum('bsd,de->bse', left, right, precision=HIGH)

def layer(entry_rows, gains, shifts, w_qkv, qv_bias, w_out, out_bias, w_up, up_bias, w_down, down_bias):
    batch_size, length, width_all = entry_rows.shape
    head_size = width_all // HEADS
    first_in = low(normalize(entry_rows, gains[0], shifts[0]))
    joined = jnp.concatenate([qv_bias[0], jnp.zeros_like(qv_bias[0]), qv_bias[1]])
    triple = low(low_back(project(first_in, w_qkv)) + joined)
    shape_heads = (batch_size, length, HEADS, head_size)
    queries = triple[..., :width_all].reshape(shape_heads)
    key_rows = triple[..., width_all:2 * width_all].reshape(shape_heads)
    value_rows = triple[..., 2 * width_all:].reshape(shape_heads)
    scores = low_back(jnp.einsum('bqhd,bkhd->bhqk', queries, key_rows, precision=HIGH) * (1.0 / math.sqrt(head_size)))
    attention = low(jax.nn.softmax(scores, axis=-1))
    mixture = jnp.einsum('bhqk,bkhd->bqhd', attention, value_rows, precision=HIGH).reshape(batch_size, length, width_all)
    mixture = low(low_back(mixture))
    middle = entry_rows + low_back(project(mixture, w_out)) + out_bias
    second_in = low(normalize(middle, gains[1], shifts[1]))
    hidden = low_back(project(second_in, w_up)) + up_bias
    active = low(jax.nn.gelu(hidden, approximate=False))
    return middle + low_back(project(active, w_down)) + down_bias

def model(patch_rows, mask_rows, mask_token, norm_gains, norm_shifts, w_qkv, qv_bias, w_out, out_bias, w_up, up_bias, w_down, down_bias):
    covered = (mask_rows == 1)[..., None]
    entry_rows = jnp.where(covered, mask_token, patch_rows)
    first_out = layer(entry_rows, norm_gains[0], norm_shifts[0], w_qkv[0], qv_bias[0], w_out[0], out_bias[0], w_up[0], up_bias[0], w_down[0], down_bias[0])
    passed = low(low_back(first_out))
    return layer(passed, norm_gains[1], norm_shifts[1], w_qkv[1], qv_bias[1], w_out[1], out_bias[1], w_up[1], up_bias[1], w_down[1], down_bias[1])

def reference(patches, block_mask, mask_token, norm_gains, norm_shifts, w_qkv, qv_bias, w_out, out_bias, w_up, up_bias, w_down, down_bias, cotangent):
    weights = tuple((item.astype(jnp.float32) for item in (mask_token, norm_gains, norm_shifts, w_qkv, qv_bias, w_out, out_bias, w_up, up_bias, w_down, down_bias)))
    groups = IMAGES // IMG_DEV
    patch_groups = patches.astype(jnp.float32).reshape(groups, IMG_DEV, SEQ, D)
    mask_groups = block_mask.reshape(groups, IMG_DEV, SEQ)
    cotangent_groups = cotangent.astype(jnp.float32).reshape(groups, IMG_DEV, SEQ, D)

    def accumulate(totals, group):
        patch_rows, mask_rows, cotangent_rows = group

        def forward(rows, *params):
            return model(rows, mask_rows, *params)
        result, pull = jax.vjp(forward, patch_rows, *weights)
        pulled = pull(cotangent_rows)
        return (tuple((total + grad for total, grad in zip(totals, pulled[1:]))), (result, pulled[0]))
    zeros = tuple((jnp.zeros_like(item) for item in weights))
    totals, outputs = lax.scan(accumulate, zeros, (patch_groups, mask_groups, cotangent_groups))
    results, patch_grads = outputs
    scale = 1.0 / math.sqrt(IMAGES * SEQ)
    boundary = jnp.stack([patch_grads.reshape(IMAGES, SEQ, D), results.reshape(IMAGES, SEQ, D)])
    return (boundary, totals[0] * scale, totals[1] * scale, totals[2] * scale, totals[3] * scale, totals[4] * scale, totals[5] * scale, totals[6] * scale, totals[7] * scale, totals[8] * scale, totals[9] * scale, totals[10] * scale)
```

```python
import functools
import math

import jax
import jax.numpy as jnp
from jax import lax
from jax.experimental import pallas as pl
from jax.experimental.pallas import tpu as pltpu
from jax.sharding import PartitionSpec as P

HEADS = 12
EPS = 1e-06
BF = jnp.bfloat16
F32 = jnp.float32
HALVINGS = (1, 2, 8, 4)
UNITS = 12
UP, OUT, QKV, DOWN_W = 4, 8, 9, 12
SMALL = 16
INV_SQRT2 = 1.0 / math.sqrt(2.0)
INV_SQRT2PI = 1.0 / math.sqrt(2.0 * math.pi)


def dot(a, b, contract_a, contract_b):
    return lax.dot_general(
        a, b, (((contract_a,), (contract_b,)), ((), ())), preferred_element_type=F32
    )


def fold8(x):
    rows, width = x.shape
    return jnp.sum(x.reshape(rows // 8, 8, width), axis=0)


def kernel(geo, *refs):
    (n, images, seq, pad, width, scale) = geo
    reduce_here = n == 16
    total_rows = images * pad
    block = width // 16
    names = ["patches", "cotangent", "mask", "token", "gains", "shifts", "qv_bias", "out_bias", "up_bias"]
    names += ["down_bias", "w_qkv", "w_out", "w_up", "w_down", "bound", "grads", "small", "wg", "x", "n1"]
    names += ["a1", "qkv", "o", "n2", "a2", "act", "gp", "dy", "send", "prob", "rstd", "mcol", "yb", "da"]
    names += ["tb", "do", "pin", "sm", "sms", "smr", "pin_sem", "w_sem", "out_sem", "fs", "fr", "bs", "br"]
    if reduce_here:
        names += ["rc", "ry", "rz", "rw", "cs", "cr", "ys", "yr", "zs", "zr", "ws", "wr", "ss", "sr"]
    r = dict(zip(names, refs, strict=True))
    wg = r["wg"]
    me = lax.axis_index("dp")
    sec = lax.axis_index("section")
    first, second = sec == 0, sec == 1

    def dp_at(bit):
        mine = lax.rem(me // bit, 2)
        return {"dp": me + bit - 2 * bit * mine, "section": sec}

    across = {"dp": me, "section": 1 - sec}
    partners = [across] + ([dp_at(bit) for bit in HALVINGS] if reduce_here else [])

    def unit_rows(unit, offset=0, size=width):
        return pl.ds(pl.multiple_of(unit * width + offset, 16), size)

    weight_copies = []
    for j in range(3):
        weight_copies.append((QKV + j, r["w_qkv"].at[0, :, pl.ds(width * j, width)]))
    weight_copies.append((OUT, r["w_out"].at[0]))
    for j in range(4):
        weight_copies.append((UP + j, r["w_up"].at[0, :, pl.ds(width * j, width)]))
    for j in range(4):
        weight_copies.append((DOWN_W + j, r["w_down"].at[0, pl.ds(width * j, width), :]))

    def weight_copy(index):
        unit, source = weight_copies[index]
        return pltpu.make_async_copy(source, wg.at[unit_rows(unit), :], r["w_sem"].at[index])

    @pl.when(first)
    def _():
        pltpu.make_async_copy(r["patches"], r["pin"], r["pin_sem"]).start()

    @pl.when(second)
    def _():
        pltpu.make_async_copy(r["cotangent"], r["pin"], r["pin_sem"]).start()

    for index in range(UNITS):
        weight_copy(index).start()

    barrier = pltpu.get_barrier_semaphore()
    for partner in partners:
        pl.semaphore_signal(barrier, inc=1, device_id=partner)
    pl.semaphore_wait(barrier, len(partners))

    r["sm"][...] = jnp.zeros_like(r["sm"])
    pltpu.make_async_copy(r["patches"], r["pin"], r["pin_sem"]).wait()

    def image_rows(img, offset=0, size=pad):
        return pl.ds(pl.multiple_of(img * pad + offset, 16), size)

    def forward_send(img):
        rows = image_rows(img)
        return pltpu.make_async_remote_copy(
            src_ref=r["send"].at[rows, :],
            dst_ref=r["x"].at[rows, :],
            send_sem=r["fs"].at[img],
            recv_sem=r["fr"].at[img],
            device_id=across,
        )

    def backward_send(img):
        rows = image_rows(img)
        return pltpu.make_async_remote_copy(
            src_ref=r["send"].at[rows, :],
            dst_ref=r["dy"].at[rows, :],
            send_sem=r["bs"].at[img],
            recv_sem=r["br"].at[img],
            device_id=across,
        )

    def bound_copy(img):
        rows = image_rows(img)
        return pltpu.make_async_copy(
            r["yb"].at[rows, :], r["bound"].at[img], r["out_sem"].at[img]
        )

    def row_blocks(img):
        return [image_rows(img, 16 * b, 16) for b in range(pad // 16)]

    def norm_forward(img, source, which, normed, scaled):
        gain = r["gains"][which : which + 1, :]
        shift = r["shifts"][which : which + 1, :]
        for rows in row_blocks(img):
            values = source[rows, :].astype(F32)
            centered = values - jnp.mean(values, axis=1, keepdims=True)
            variance = jnp.mean(centered * centered, axis=1, keepdims=True)
            inverse = lax.rsqrt(variance + EPS)
            unit = centered * inverse
            r["rstd"][which, rows, :] = inverse
            normed[rows, :] = unit.astype(BF)
            scaled[rows, :] = (unit * gain + shift).astype(BF)

    def halves(values):
        lane = lax.broadcasted_iota(jnp.int32, values.shape, 1)
        zero = jnp.zeros_like(values)
        low = lane < width // HEADS
        return jnp.where(low, values, zero), jnp.where(low, zero, values)

    def attention_forward(img, pair):
        rows = image_rows(img)
        lanes = pl.ds(pl.multiple_of(128 * pair, 128), 128)
        queries = r["qkv"][0, rows, lanes]
        keys = r["qkv"][1, rows, lanes]
        values = r["qkv"][2, rows, lanes]
        mixed = []
        for head, part in enumerate(halves(queries)):
            scores = dot(keys, part, 1, 1)
            key_at = lax.broadcasted_iota(jnp.int32, scores.shape, 0)
            scores = jnp.where(key_at < seq, scores, -1e30)
            raised = jnp.exp(scores - jnp.max(scores, axis=0, keepdims=True))
            share = 1.0 / jnp.sum(raised, axis=0, keepdims=True)
            prob = (raised * share).astype(BF)
            r["prob"][img * HEADS + 2 * pair + head] = prob
            mixed.append(dot(prob, values, 0, 0))
        lane = lax.broadcasted_iota(jnp.int32, mixed[0].shape, 1)
        r["o"][rows, lanes] = jnp.where(lane < width // HEADS, mixed[0], mixed[1]).astype(BF)

    def wait_weights(step, indices):
        @pl.when(step == 0)
        def _():
            for index in indices:
                weight_copy(index).wait()

    def forward(step, img):
        rows = image_rows(img)

        @pl.when(first)
        def _():
            tail = image_rows(img, seq // 16 * 16, 16)
            r["x"][tail, :] = jnp.zeros((16, width), BF)
            row = r["mask"][pl.ds(img, 1), :]
            at_row = lax.broadcasted_iota(jnp.int32, (pad, seq), 0)
            at_lane = lax.broadcasted_iota(jnp.int32, (pad, seq), 1)
            covered = jnp.where((at_row == at_lane) & (row == 1), 1.0, 0.0)
            column = jnp.sum(covered, axis=1, keepdims=True)
            r["mcol"][rows, :] = column
            token = r["token"][...].astype(F32)
            kept = r["pin"][img].astype(F32)
            mixed = jnp.where(column[:seq] > 0.5, token, kept)
            r["x"][image_rows(img, 0, seq), :] = mixed.astype(BF)

        @pl.when(second)
        def _():
            forward_send(img).wait_recv()

        norm_forward(img, r["x"], 0, r["n1"], r["a1"])
        wait_weights(step, range(0, 3))
        for j in range(3):
            projected = dot(r["a1"][rows, :], wg[unit_rows(QKV + j), :], 1, 0)
            if j == 0:
                projected = (projected + r["qv_bias"][0:1, :]) * (1.0 / math.sqrt(width // HEADS))
            if j == 2:
                projected = projected + r["qv_bias"][1:2, :]
            r["qkv"][j, rows, :] = projected.astype(BF)

        def three_pairs(half, carry):
            for pair in range(HEADS // 4):
                attention_forward(img, half * (HEADS // 4) + pair)
            return carry

        lax.fori_loop(0, 2, three_pairs, 0)
        wait_weights(step, range(3, UNITS))
        r["yb"][rows, :] = (
            r["x"][rows, :].astype(F32)
            + dot(r["o"][rows, :], wg[unit_rows(OUT), :], 1, 0)
            + r["out_bias"][...]
        )
        norm_forward(img, r["yb"], 1, r["n2"], r["a2"])
        result = None
        for j in range(4):
            hidden = dot(r["a2"][rows, :], wg[unit_rows(UP + j), :], 1, 0)
            hidden = hidden + r["up_bias"][:, width * j : width * (j + 1)]
            below = 0.5 + 0.5 * lax.erf(hidden * INV_SQRT2)
            slope = below + hidden * (jnp.exp(hidden * hidden * -0.5) * INV_SQRT2PI)
            active = (hidden * below).astype(BF)
            r["act"][j, rows, :] = active
            r["gp"][j, rows, :] = slope.astype(BF)
            term = dot(active, wg[unit_rows(DOWN_W + j), :], 1, 0)
            result = term if result is None else result + term
        r["yb"][rows, :] = r["yb"][rows, :] + result + r["down_bias"][...]

        @pl.when(first)
        def _():
            r["send"][rows, :] = r["yb"][rows, :].astype(BF)
            forward_send(img).start()

        @pl.when(second)
        def _():
            bound_copy(img).start()

    def take_gradient(img):
        @pl.when(first)
        def _():
            backward_send(img).wait_recv()

        @pl.when(second)
        def _():
            tail = image_rows(img, seq // 16 * 16, 16)
            r["dy"][tail, :] = jnp.zeros((16, width), BF)
            r["dy"][image_rows(img, 0, seq), :] = r["pin"][img]

    def norm_backward(img, which, gradient, incoming):
        gain = r["gains"][which : which + 1, :]
        normed = r["n1"] if which == 0 else r["n2"]
        gain_sum = jnp.zeros((8, width), F32)
        shift_sum = jnp.zeros((8, width), F32)
        for b, rows in enumerate(row_blocks(img)):
            here = gradient[16 * b : 16 * (b + 1), :]
            unit = normed[rows, :].astype(F32)
            gain_sum = gain_sum + fold8(here * unit)
            shift_sum = shift_sum + fold8(here)
            scaled = here * gain
            mean = jnp.mean(scaled, axis=1, keepdims=True)
            along = jnp.mean(scaled * unit, axis=1, keepdims=True)
            local = (scaled - mean - unit * along) * r["rstd"][which, rows, :]
            yield b, rows, local + incoming(b, rows)
        r["sm"][which : which + 1, :] += jnp.sum(gain_sum, axis=0, keepdims=True)
        r["sm"][2 + which : 3 + which, :] += jnp.sum(shift_sum, axis=0, keepdims=True)

    def backward_mlp(img):
        rows = image_rows(img)
        incoming = r["dy"][rows, :]
        r["sm"][11:12, :] += jnp.sum(incoming.astype(F32), axis=0, keepdims=True)
        back = None
        for j in range(4):
            change = dot(incoming, wg[unit_rows(DOWN_W + j), :], 1, 1)
            change = change * r["gp"][j, rows, :].astype(F32)
            r["sm"][7 + j : 8 + j, :] += jnp.sum(change, axis=0, keepdims=True)
            narrow = change.astype(BF)
            r["gp"][j, rows, :] = narrow
            term = dot(narrow, wg[unit_rows(UP + j), :], 1, 1)
            back = term if back is None else back + term
        r["tb"][...] = back
        bias_sum = jnp.zeros((8, width), F32)
        for b, block_rows, middle in norm_backward(
            img, 1, r["tb"], lambda b, block_rows: r["dy"][block_rows, :].astype(F32)
        ):
            bias_sum = bias_sum + fold8(middle)
            r["da"][16 * b : 16 * (b + 1), :] = middle
            r["n2"][block_rows, :] = middle.astype(BF)
        r["sm"][6:7, :] += jnp.sum(bias_sum, axis=0, keepdims=True)

    def attention_backward(img, pair):
        rows = image_rows(img)
        lanes = pl.ds(pl.multiple_of(128 * pair, 128), 128)
        queries = halves(r["qkv"][0, rows, lanes])
        keys = r["qkv"][1, rows, lanes]
        values = r["qkv"][2, rows, lanes]
        back = halves(r["do"][:, lanes])
        key_parts = halves(keys)
        d_query = d_key = d_value = None
        for head in range(2):
            prob = r["prob"][img * HEADS + 2 * pair + head]
            wide = prob.astype(F32)
            change = dot(values, back[head], 1, 1)
            carried = jnp.sum(wide * change, axis=0, keepdims=True)
            scores = (wide * (change - carried)).astype(BF)
            terms = (
                dot(scores, key_parts[head], 0, 0),
                dot(scores, queries[head], 1, 0),
                dot(prob, back[head], 1, 0),
            )
            if head == 0:
                d_query, d_key, d_value = terms
            else:
                d_query, d_key, d_value = d_query + terms[0], d_key + terms[1], d_value + terms[2]
        d_query = d_query * (1.0 / math.sqrt(width // HEADS))
        r["sm"][4:5, lanes] += jnp.sum(d_query, axis=0, keepdims=True)
        r["sm"][5:6, lanes] += jnp.sum(d_value, axis=0, keepdims=True)
        r["qkv"][0, rows, lanes] = d_query.astype(BF)
        r["qkv"][1, rows, lanes] = d_key.astype(BF)
        r["qkv"][2, rows, lanes] = d_value.astype(BF)

    def backward_attention(img):
        rows = image_rows(img)
        r["do"][...] = dot(r["n2"][rows, :], wg[unit_rows(OUT), :], 1, 1).astype(BF)

        def three_pairs(half, carry):
            for pair in range(HEADS // 4):
                attention_backward(img, half * (HEADS // 4) + pair)
            return carry

        lax.fori_loop(0, 2, three_pairs, 0)
        back = None
        for j in range(3):
            term = dot(r["qkv"][j, rows, :], wg[unit_rows(QKV + j), :], 1, 1)
            back = term if back is None else back + term
        r["tb"][...] = back
        for b, block_rows, entry in norm_backward(
            img, 0, r["tb"], lambda b, block_rows: r["da"][16 * b : 16 * (b + 1), :]
        ):
            r["da"][16 * b : 16 * (b + 1), :] = entry

        @pl.when(first)
        def _():
            token_sum = jnp.zeros((8, width), F32)
            for b, block_rows in enumerate(row_blocks(img)):
                entry = r["da"][16 * b : 16 * (b + 1), :]
                under = r["mcol"][block_rows, :] > 0.5
                token_sum = token_sum + fold8(jnp.where(under, entry, 0.0))
                r["yb"][block_rows, :] = jnp.where(under, 0.0, entry)
            r["sm"][12:13, :] += jnp.sum(token_sum, axis=0, keepdims=True)
            bound_copy(img).start()

        @pl.when(second)
        def _():
            r["send"][rows, :] = r["da"][...].astype(BF)
            backward_send(img).start()

    if reduce_here:
        mine = [lax.rem(me // bit, 2) for bit in HALVINGS]
        landing = [r["rc"], r["ry"], r["rz"], r["rw"]]
        sends = [r["cs"], r["ys"], r["zs"], r["ws"]]
        arrivals = [r["cr"], r["yr"], r["zr"], r["wr"]]

    def kept_offset(steps):
        offset = 0
        for s in range(steps):
            offset = offset + mine[s] * (width >> (s + 1))
        return offset

    def halving(s, unit):
        size = width >> (s + 1)
        away = kept_offset(s) + (1 - mine[s]) * size
        return pltpu.make_async_remote_copy(
            src_ref=wg.at[unit_rows(unit, away, size), :],
            dst_ref=landing[s].at[pl.ds(pl.multiple_of(unit * size, 16), size), :],
            send_sem=sends[s].at[unit],
            recv_sem=arrivals[s].at[unit],
            device_id=dp_at(HALVINGS[s]),
        )

    def add_arrived(s, unit):
        size = width >> (s + 1)
        halving(s, unit).wait_recv()
        here = kept_offset(s + 1)
        for part in range(size // 48):
            rows = unit_rows(unit, here + 48 * part, 48)
            came = landing[s][pl.ds(pl.multiple_of(unit * size + 48 * part, 16), 48), :]
            both = wg[rows, :].astype(F32) + came.astype(F32)
            if s < 3:
                wg[rows, :] = both.astype(BF)
            else:
                r["grads"][unit] = both * scale
        if s < 3:
            halving(s + 1, unit).start()

    def place(owner):
        where = 0
        for s, bit in enumerate(HALVINGS):
            where = where + lax.rem(owner // bit, 2) * (8 >> s)
        return where

    def weight_gradient(left, right, chunk, first_unit, spread):
        for half in range(2):
            product = dot(left(half), right, 0, 0).astype(BF)
            for b in range(8):
                at = chunk * 16 + 8 * half + b
                if reduce_here:
                    owner, part = at // spread, lax.rem(at, spread)
                    rows = unit_rows(first_unit + part, place(owner) * block, block)
                else:
                    rows = unit_rows(first_unit, at * block, block)
                wg[rows, :] = product[block * b : block * (b + 1), :]

    def half_lanes(half):
        return pl.ds((width // 2) * half, width // 2)

    def down_gradient():
        def one(j, carry):
            weight_gradient(lambda half: r["dy"][:, half_lanes(half)], r["act"][j], 0, j, 1)
            if reduce_here:
                halving(0, j).start()
            return carry

        lax.fori_loop(0, 4, one, 0)

    def start_units(begin, end):
        if reduce_here:
            for unit in range(begin, end):
                halving(0, unit).start()

    def add_units(s, begin, end):
        if reduce_here:

            def one(unit, carry):
                add_arrived(s, unit)
                return carry

            lax.fori_loop(begin, end, one, 0)

    def turn(step, carry):
        img = lax.rem(step, images)
        early = step < images
        back_now = early == second
        down_now = step == jnp.where(first, 2 * images - 1, images)

        @pl.when(early)
        def _():
            forward(step, img)

        @pl.when(back_now)
        def _():
            take_gradient(img)

        @pl.when(down_now)
        def _():
            down_gradient()

        @pl.when(back_now)
        def _():
            backward_mlp(img)

        @pl.when(down_now)
        def _():
            add_units(0, 0, 4)

        @pl.when(back_now)
        def _():
            backward_attention(img)

        return carry

    lax.fori_loop(0, 2 * images, turn, 0)

    def up_one(c, carry):
        weight_gradient(lambda half: r["gp"][c, :, half_lanes(half)], r["a2"][...], c, UP, 4)
        return carry

    lax.fori_loop(0, 4, up_one, 0)
    start_units(UP, OUT)
    weight_gradient(lambda half: r["n2"][:, half_lanes(half)], r["o"][...], 0, OUT, 1)
    start_units(OUT, QKV)
    add_units(0, UP, OUT)

    def qkv_one(c, carry):
        weight_gradient(lambda half: r["qkv"][c, :, half_lanes(half)], r["a1"][...], c, QKV, 3)
        return carry

    lax.fori_loop(0, 3, qkv_one, 0)
    start_units(QKV, UNITS)
    add_units(0, OUT, UNITS)

    if reduce_here:
        hops = [dp_at(bit) for bit in HALVINGS] + [across]

        def small_send(t):
            return pltpu.make_async_remote_copy(
                src_ref=r["sms"].at[t],
                dst_ref=r["smr"].at[t],
                send_sem=r["ss"].at[t],
                recv_sem=r["sr"].at[t],
                device_id=hops[t],
            )

        r["sms"][0] = r["sm"][...]
        small_send(0).start()

        def drain(k, carry):
            @pl.when(k < UNITS)
            def _():
                add_arrived(1, k)

            for t in range(5):

                @pl.when(k == t + 1)
                def _(t=t):
                    small_send(t).wait_recv()
                    if t < 3:
                        r["sms"][t + 1] = r["sms"][t] + r["smr"][t]
                        small_send(t + 1).start()
                    elif t == 3:
                        r["sms"][4] = r["sms"][3] + r["smr"][3]
                        small_send(4).start()
                    else:
                        r["small"][0:12, :] = r["sms"][4, 0:12, :] * scale
                        r["small"][12:SMALL, :] = (
                            r["sms"][4, 12:SMALL, :] + r["smr"][4, 12:SMALL, :]
                        ) * scale

            @pl.when((k >= 1) & (k < UNITS + 1))
            def _():
                add_arrived(2, k - 1)

            @pl.when(k >= 2)
            def _():
                add_arrived(3, k - 2)

            return carry

        lax.fori_loop(0, UNITS + 2, drain, 0)

        def sent(unit, carry):
            for s in range(4):
                halving(s, unit).wait_send()
            return carry

        lax.fori_loop(0, UNITS, sent, 0)
        for t in range(5):
            small_send(t).wait_send()
    else:
        r["small"][...] = r["sm"][...] * scale
        out = pltpu.make_async_copy(wg.at[pl.ds(0, UNITS * width), :], r["grads"], r["pin_sem"])
        out.start()
        out.wait()

    for img in range(images):
        bound_copy(img).wait()

        @pl.when(first)
        def _(img=img):
            forward_send(img).wait_send()

        @pl.when(second)
        def _(img=img):
            backward_send(img).wait_send()


def on_device(n, *args):
    (patches, block_mask, mask_token, norm_gains, norm_shifts, w_qkv, qv_bias, w_out, out_bias) = args[:9]
    w_up, up_bias, w_down, down_bias, cotangent = args[9:]
    images, seq, width = patches.shape
    pad = -(-seq // 16) * 16
    rows = images * pad
    reduce_here = n == 16
    scale = 1.0 / math.sqrt(images * n * seq)
    geo = (n, images, seq, pad, width, scale)
    block = width // 16
    anywhere = pl.BlockSpec(memory_space=pl.ANY)
    vmem = pl.BlockSpec(memory_space=pltpu.VMEM)
    if reduce_here:
        grads_shape = jax.ShapeDtypeStruct((UNITS, block, width), F32)
    else:
        grads_shape = jax.ShapeDtypeStruct((UNITS * width, width), BF)
    narrow = pltpu.VMEM((rows, width), BF)
    dma = pltpu.SemaphoreType.DMA
    scratch = [
        pltpu.VMEM((16 * width, width), BF),
        narrow,
        narrow,
        narrow,
        pltpu.VMEM((3, rows, width), BF),
        narrow,
        narrow,
        narrow,
        pltpu.VMEM((4, rows, width), BF),
        pltpu.VMEM((4, rows, width), BF),
        narrow,
        narrow,
        pltpu.VMEM((images * HEADS, pad, pad), BF),
        pltpu.VMEM((2, rows, 1), F32),
        pltpu.VMEM((rows, 1), F32),
        pltpu.VMEM((rows, width), F32),
        pltpu.VMEM((pad, width), F32),
        pltpu.VMEM((pad, width), F32),
        pltpu.VMEM((pad, width), BF),
        pltpu.VMEM((images, seq, width), BF),
        pltpu.VMEM((SMALL, width), F32),
        pltpu.VMEM((5, SMALL, width), F32),
        pltpu.VMEM((5, SMALL, width), F32),
        dma(()),
        dma((UNITS,)),
        dma((images,)),
        dma((images,)),
        dma((images,)),
        dma((images,)),
        dma((images,)),
    ]
    if reduce_here:
        scratch += [pltpu.VMEM((UNITS * (width >> (s + 1)), width), BF) for s in range(4)]
        scratch += [dma((UNITS,))] * 8 + [dma((5,))] * 2
    weights = 12 * width * width
    bound, grads, small = pl.pallas_call(
        functools.partial(kernel, geo),
        out_shape=(
            jax.ShapeDtypeStruct((images, pad, width), F32),
            grads_shape,
            jax.ShapeDtypeStruct((SMALL, width), F32),
        ),
        in_specs=[anywhere] * 2 + [vmem] * 8 + [anywhere] * 4,
        out_specs=(anywhere, vmem if reduce_here else anywhere, vmem),
        scratch_shapes=scratch,
        compiler_params=pltpu.CompilerParams(
            collective_id=0, has_side_effects=True, vmem_limit_bytes=64 * 1024 * 1024 - 65536
        ),
        cost_estimate=pl.CostEstimate(
            flops=6 * rows * weights, bytes_accessed=4 * weights, transcendentals=rows * width * 8
        ),
        name="relay",
    )(
        patches,
        cotangent,
        block_mask,
        mask_token[None],
        norm_gains[0],
        norm_shifts[0],
        qv_bias[0],
        out_bias,
        up_bias,
        down_bias,
        w_qkv,
        w_out,
        w_up,
        w_down,
    )
    me = lax.axis_index("dp")
    boundary = bound[:, :seq][None]
    share = width // n
    if reduce_here:
        token = small[12]
        vectors = small[:12]
        down = grads[:4].transpose(0, 2, 1).reshape(4 * width, share)
        up = grads[4:8].transpose(2, 0, 1).reshape(width, 4 * share)
        out = grads[8].T
        qkv = grads[9:].transpose(2, 0, 1).reshape(width, 3 * share)
    else:
        token = lax.psum(small[12], ("dp", "section"))
        vectors = lax.psum(small[:12], "dp")
        wide = grads.astype(F32) * scale

        def scattered(first, count):
            part = wide[first * width : (first + count) * width]
            return lax.psum_scatter(part, "dp", scatter_dimension=0, tiled=True).T

        down = lax.psum_scatter(
            wide[: 4 * width].reshape(4, width, width), "dp", scatter_dimension=1, tiled=True
        )
        down = down.transpose(0, 2, 1).reshape(4 * width, share)
        up = scattered(UP, 4)
        out = scattered(OUT, 1)
        qkv = scattered(QKV, 3)

    def cut(first, count):
        return lax.dynamic_slice(vectors, (first, me * share), (count, share))

    up_vector = lax.dynamic_slice(vectors[7:11].reshape(-1), (me * 4 * share,), (4 * share,))
    return (
        boundary,
        token,
        cut(0, 2)[None],
        cut(2, 2)[None],
        qkv[None],
        cut(4, 2)[None],
        out[None],
        cut(6, 1),
        up[None],
        up_vector[None],
        down[None],
        cut(11, 1),
    )


def solution(mesh):
    return jax.shard_map(
        functools.partial(on_device, mesh.shape["dp"]),
        mesh=mesh,
        in_specs=(
            P("dp", None, None),
            P("dp", None),
            P(),
            P("section", None, None),
            P("section", None, None),
            P("section", None, None),
            P("section", None, None),
            P("section", None, None),
            P("section", None),
            P("section", None, None),
            P("section", None),
            P("section", None, None),
            P("section", None),
            P("dp", None, None),
        ),
        out_specs=(
            P("section", "dp", None, None),
            P(),
            P("section", None, "dp"),
            P("section", None, "dp"),
            P("section", None, "dp"),
            P("section", None, "dp"),
            P("section", None, "dp"),
            P("section", "dp"),
            P("section", None, "dp"),
            P("section", "dp"),
            P("section", None, "dp"),
            P("section", "dp"),
        ),
        check_vma=False,
    )
```

```python
import functools
import math

import jax
import jax.numpy as jnp
from jax import lax
from jax.experimental import pallas as pl
from jax.experimental.pallas import tpu as pltpu
from jax.sharding import PartitionSpec as P

HEADS = 12
EPS = 1e-06
BF = jnp.bfloat16
F32 = jnp.float32
Z_FIRST = (2, 4)
WINDOW = 2
UNITS = 12
UP, OUT, QKV, DOWN_W = 4, 8, 9, 12
SMALL = 16
INV_SQRT2 = 1.0 / math.sqrt(2.0)
INV_SQRT2PI = 1.0 / math.sqrt(2.0 * math.pi)


def dot(a, b, contract_a, contract_b):
    return lax.dot_general(
        a, b, (((contract_a,), (contract_b,)), ((), ())), preferred_element_type=F32
    )


def fold8(x):
    rows, width = x.shape
    return jnp.sum(x.reshape(rows // 8, 8, width), axis=0)


def kernel(geo, *refs):
    (n, images, seq, pad, width, scale) = geo
    reduce_here = n == 16
    total_rows = images * pad
    block = width // 16
    names = ["patches", "cotangent", "mask", "token", "gains", "shifts", "qv_bias", "out_bias", "up_bias"]
    names += ["down_bias", "w_qkv", "w_out", "w_up", "w_down", "bound"]
    if reduce_here:
        names += ["down", "up", "out", "three", "g_gains", "g_shifts", "g_qv", "g_out", "g_up", "g_down"]
        names += ["g_token"]
    else:
        names += ["grads", "small"]
    names += ["wg", "x", "n1", "a1", "qkv", "o", "n2", "a2", "act", "gp", "dy", "send", "prob", "cols"]
    names += ["yb", "da", "tb", "do", "pin", "plain", "sm", "sms", "smr"]
    names += ["pin_sem", "w_sem", "out_sem", "fs", "fr", "bs", "br"]
    if reduce_here:
        names += ["rc", "ry", "zb", "zf", "cs", "cr", "ys", "yr", "rs", "rr", "ls", "lr", "ss", "sr"]
    r = dict(zip(names, refs, strict=True))
    wg = r["wg"]
    me = lax.axis_index("dp")
    sec = lax.axis_index("section")
    first, second = sec == 0, sec == 1

    def dp_at(bit):
        mine = lax.rem(me // bit, 2)
        return {"dp": me + bit - 2 * bit * mine, "section": sec}

    across = {"dp": me, "section": 1 - sec}
    core, y_at, z_at = lax.rem(me, 2), lax.rem(me // 2, 2), me // 4
    partners = [across]
    if reduce_here:
        partners += [dp_at(1), dp_at(2)]
        partners += [{"dp": lax.rem(me + 4 * turn, n), "section": sec} for turn in (1, 2, 3)]

    def unit_rows(unit, offset=0, size=width):
        return pl.ds(pl.multiple_of(unit * width + offset, 16), size)

    weight_copies = []
    for j in range(3):
        weight_copies.append((QKV + j, r["w_qkv"].at[0, :, pl.ds(width * j, width)]))
    weight_copies.append((OUT, r["w_out"].at[0]))
    for j in range(4):
        weight_copies.append((UP + j, r["w_up"].at[0, :, pl.ds(width * j, width)]))
    for j in range(4):
        weight_copies.append((DOWN_W + j, r["w_down"].at[0, pl.ds(width * j, width), :]))

    def weight_copy(index):
        unit, source = weight_copies[index]
        return pltpu.make_async_copy(source, wg.at[unit_rows(unit), :], r["w_sem"].at[index])

    @pl.when(first)
    def _():
        pltpu.make_async_copy(r["patches"], r["pin"], r["pin_sem"]).start()

    @pl.when(second)
    def _():
        pltpu.make_async_copy(r["cotangent"], r["pin"], r["pin_sem"]).start()

    for index in range(UNITS):
        weight_copy(index).start()

    barrier = pltpu.get_barrier_semaphore()
    for partner in partners:
        pl.semaphore_signal(barrier, inc=1, device_id=partner)
    pl.semaphore_wait(barrier, len(partners))

    r["sm"][...] = jnp.zeros_like(r["sm"])
    pltpu.make_async_copy(r["patches"], r["pin"], r["pin_sem"]).wait()

    def image_rows(img, offset=0, size=pad):
        return pl.ds(pl.multiple_of(img * pad + offset, 16), size)

    def forward_send(img):
        rows = image_rows(img)
        return pltpu.make_async_remote_copy(
            src_ref=r["send"].at[rows, :],
            dst_ref=r["x"].at[rows, :],
            send_sem=r["fs"].at[img],
            recv_sem=r["fr"].at[img],
            device_id=across,
        )

    def backward_send(img):
        rows = image_rows(img)
        return pltpu.make_async_remote_copy(
            src_ref=r["send"].at[rows, :],
            dst_ref=r["dy"].at[rows, :],
            send_sem=r["bs"].at[img],
            recv_sem=r["br"].at[img],
            device_id=across,
        )

    def bound_copy(img):
        return pltpu.make_async_copy(r["plain"].at[img], r["bound"].at[img], r["out_sem"].at[img])

    def write_bound(img, at, values):
        size = min(16, seq - at)
        r["plain"][img, at : at + size, 0, :] = values[:size]

    def row_blocks(img):
        return [image_rows(img, 16 * b, 16) for b in range(pad // 16)]

    def norm_forward(img, read, which, normed, scaled):
        gain = r["gains"][which : which + 1, :]
        shift = r["shifts"][which : which + 1, :]
        for b, rows in enumerate(row_blocks(img)):
            values = read(b, rows)
            centered = values - jnp.mean(values, axis=1, keepdims=True)
            variance = jnp.mean(centered * centered, axis=1, keepdims=True)
            inverse = lax.rsqrt(variance + EPS)
            unit = centered * inverse
            r["cols"][rows, which : which + 1] = inverse
            normed[rows, :] = unit.astype(BF)
            scaled[rows, :] = (unit * gain + shift).astype(BF)

    def halves(values):
        lane = lax.broadcasted_iota(jnp.int32, values.shape, 1)
        zero = jnp.zeros_like(values)
        low = lane < width // HEADS
        return jnp.where(low, values, zero), jnp.where(low, zero, values)

    def attention_forward(img, pair):
        rows = image_rows(img)
        lanes = pl.ds(pl.multiple_of(128 * pair, 128), 128)
        queries = r["qkv"][0, rows, lanes]
        keys = r["qkv"][1, rows, lanes]
        values = r["qkv"][2, rows, lanes]
        mixed = []
        for head, part in enumerate(halves(queries)):
            scores = dot(keys, part, 1, 1)
            key_at = lax.broadcasted_iota(jnp.int32, scores.shape, 0)
            scores = jnp.where(key_at < seq, scores, -1e30)
            raised = jnp.exp(scores - jnp.max(scores, axis=0, keepdims=True))
            share = 1.0 / jnp.sum(raised, axis=0, keepdims=True)
            prob = (raised * share).astype(BF)
            r["prob"][img * HEADS + 2 * pair + head] = prob
            mixed.append(dot(prob, values, 0, 0))
        lane = lax.broadcasted_iota(jnp.int32, mixed[0].shape, 1)
        r["o"][rows, lanes] = jnp.where(lane < width // HEADS, mixed[0], mixed[1]).astype(BF)

    def wait_weights(step, indices):
        @pl.when(step == 0)
        def _():
            for index in indices:
                weight_copy(index).wait()

    def forward(step, img):
        rows = image_rows(img)

        @pl.when(first)
        def _():
            tail = image_rows(img, seq // 16 * 16, 16)
            r["x"][tail, :] = jnp.zeros((16, width), BF)
            row = r["mask"][pl.ds(img, 1), :]
            at_row = lax.broadcasted_iota(jnp.int32, (pad, seq), 0)
            at_lane = lax.broadcasted_iota(jnp.int32, (pad, seq), 1)
            covered = jnp.where((at_row == at_lane) & (row == 1), 1.0, 0.0)
            column = jnp.sum(covered, axis=1, keepdims=True)
            r["cols"][rows, 2:3] = column
            token = r["token"][...][None, :].astype(F32)
            kept = r["pin"][img].astype(F32)
            mixed = jnp.where(column[:seq] > 0.5, token, kept)
            r["x"][image_rows(img, 0, seq), :] = mixed.astype(BF)

        @pl.when(second)
        def _():
            forward_send(img).wait_recv()

        norm_forward(img, lambda b, at: r["x"][at, :].astype(F32), 0, r["n1"], r["a1"])
        wait_weights(step, range(0, 3))
        for j in range(3):
            projected = dot(r["a1"][rows, :], wg[unit_rows(QKV + j), :], 1, 0)
            if j == 0:
                projected = (projected + r["qv_bias"][0:1, :]) * (1.0 / math.sqrt(width // HEADS))
            if j == 2:
                projected = projected + r["qv_bias"][1:2, :]
            r["qkv"][j, rows, :] = projected.astype(BF)

        def three_pairs(half, carry):
            for pair in range(HEADS // 4):
                attention_forward(img, half * (HEADS // 4) + pair)
            return carry

        lax.fori_loop(0, 2, three_pairs, 0)
        wait_weights(step, range(3, UNITS))
        r["yb"][...] = (
            r["x"][rows, :].astype(F32)
            + dot(r["o"][rows, :], wg[unit_rows(OUT), :], 1, 0)
            + r["out_bias"][...]
        )
        norm_forward(img, lambda b, at: r["yb"][16 * b : 16 * (b + 1), :], 1, r["n2"], r["a2"])
        result = None
        for j in range(4):
            hidden = dot(r["a2"][rows, :], wg[unit_rows(UP + j), :], 1, 0)
            hidden = hidden + r["up_bias"][:, width * j : width * (j + 1)]
            below = 0.5 + 0.5 * lax.erf(hidden * INV_SQRT2)
            slope = below + hidden * (jnp.exp(hidden * hidden * -0.5) * INV_SQRT2PI)
            active = (hidden * below).astype(BF)
            r["act"][j, rows, :] = active
            r["gp"][j, rows, :] = slope.astype(BF)
            term = dot(active, wg[unit_rows(DOWN_W + j), :], 1, 0)
            result = term if result is None else result + term
        result = r["yb"][...] + result + r["down_bias"][...]

        @pl.when(first)
        def _():
            r["send"][rows, :] = result.astype(BF)
            forward_send(img).start()

        @pl.when(second)
        def _():
            for at in range(0, seq, 16):
                write_bound(img, at, result[at : at + 16])

    def take_gradient(img):
        @pl.when(first)
        def _():
            backward_send(img).wait_recv()

        @pl.when(second)
        def _():
            tail = image_rows(img, seq // 16 * 16, 16)
            r["dy"][tail, :] = jnp.zeros((16, width), BF)
            r["dy"][image_rows(img, 0, seq), :] = r["pin"][img]

    def norm_backward(img, which, gradient, incoming):
        gain = r["gains"][which : which + 1, :]
        normed = r["n1"] if which == 0 else r["n2"]
        gain_sum = jnp.zeros((8, width), F32)
        shift_sum = jnp.zeros((8, width), F32)
        for b, rows in enumerate(row_blocks(img)):
            here = gradient[16 * b : 16 * (b + 1), :]
            unit = normed[rows, :].astype(F32)
            gain_sum = gain_sum + fold8(here * unit)
            shift_sum = shift_sum + fold8(here)
            scaled = here * gain
            mean = jnp.mean(scaled, axis=1, keepdims=True)
            along = jnp.mean(scaled * unit, axis=1, keepdims=True)
            local = (scaled - mean - unit * along) * r["cols"][rows, which : which + 1]
            yield b, rows, local + incoming(b, rows)
        r["sm"][which : which + 1, :] += jnp.sum(gain_sum, axis=0, keepdims=True)
        r["sm"][2 + which : 3 + which, :] += jnp.sum(shift_sum, axis=0, keepdims=True)

    def backward_mlp(img):
        rows = image_rows(img)
        incoming = r["dy"][rows, :]
        r["sm"][11:12, :] += jnp.sum(incoming.astype(F32), axis=0, keepdims=True)
        back = None
        for j in range(4):
            change = dot(incoming, wg[unit_rows(DOWN_W + j), :], 1, 1)
            change = change * r["gp"][j, rows, :].astype(F32)
            r["sm"][7 + j : 8 + j, :] += jnp.sum(change, axis=0, keepdims=True)
            narrow = change.astype(BF)
            r["gp"][j, rows, :] = narrow
            term = dot(narrow, wg[unit_rows(UP + j), :], 1, 1)
            back = term if back is None else back + term
        r["tb"][...] = back
        bias_sum = jnp.zeros((8, width), F32)
        for b, block_rows, middle in norm_backward(
            img, 1, r["tb"], lambda b, block_rows: r["dy"][block_rows, :].astype(F32)
        ):
            bias_sum = bias_sum + fold8(middle)
            r["da"][16 * b : 16 * (b + 1), :] = middle
            r["n2"][block_rows, :] = middle.astype(BF)
        r["sm"][6:7, :] += jnp.sum(bias_sum, axis=0, keepdims=True)

    def attention_backward(img, pairs):
        rows = image_rows(img)
        places = [pl.ds(pl.multiple_of(128 * pair, 128), 128) for pair in pairs]
        loaded = []
        for pair, lanes in zip(pairs, places):
            probs = [r["prob"][img * HEADS + 2 * pair + head] for head in range(2)]
            loaded.append((*[r["qkv"][i, rows, lanes] for i in range(3)], r["do"][:, lanes], probs))
        results = []
        for queries, keys, values, back, probs in loaded:
            query_parts, key_parts, back_parts = halves(queries), halves(keys), halves(back)
            total = None
            for head in range(2):
                wide = probs[head].astype(F32)
                change = dot(values, back_parts[head], 1, 1)
                carried = jnp.sum(wide * change, axis=0, keepdims=True)
                scores = (wide * (change - carried)).astype(BF)
                terms = (
                    dot(scores, key_parts[head], 0, 0),
                    dot(scores, query_parts[head], 1, 0),
                    dot(probs[head], back_parts[head], 1, 0),
                )
                total = terms if total is None else [a + b for a, b in zip(total, terms)]
            d_query, d_key, d_value = total
            results.append((d_query * (1.0 / math.sqrt(width // HEADS)), d_key, d_value))
        for (d_query, d_key, d_value), lanes in zip(results, places):
            r["sm"][4:5, lanes] += jnp.sum(d_query, axis=0, keepdims=True)
            r["sm"][5:6, lanes] += jnp.sum(d_value, axis=0, keepdims=True)
            r["qkv"][0, rows, lanes] = d_query.astype(BF)
            r["qkv"][1, rows, lanes] = d_key.astype(BF)
            r["qkv"][2, rows, lanes] = d_value.astype(BF)

    def backward_attention(img):
        rows = image_rows(img)
        r["do"][...] = dot(r["n2"][rows, :], wg[unit_rows(OUT), :], 1, 1).astype(BF)

        def three_pairs(half, carry):
            attention_backward(img, [half * (HEADS // 4) + pair for pair in range(HEADS // 4)])
            return carry

        lax.fori_loop(0, 2, three_pairs, 0)
        back = None
        for j in range(3):
            term = dot(r["qkv"][j, rows, :], wg[unit_rows(QKV + j), :], 1, 1)
            back = term if back is None else back + term
        r["tb"][...] = back
        for b, block_rows, entry in norm_backward(
            img, 0, r["tb"], lambda b, block_rows: r["da"][16 * b : 16 * (b + 1), :]
        ):
            r["da"][16 * b : 16 * (b + 1), :] = entry

        @pl.when(first)
        def _():
            token_sum = jnp.zeros((8, width), F32)
            for b, block_rows in enumerate(row_blocks(img)):
                entry = r["da"][16 * b : 16 * (b + 1), :]
                under = r["cols"][block_rows, 2:3] > 0.5
                token_sum = token_sum + fold8(jnp.where(under, entry, 0.0))
                if 16 * b < seq:
                    write_bound(img, 16 * b, jnp.where(under, 0.0, entry))
            r["sm"][12:13, :] += jnp.sum(token_sum, axis=0, keepdims=True)

        @pl.when(second)
        def _():
            r["send"][rows, :] = r["da"][...].astype(BF)
            backward_send(img).start()

    half_rows, quarter = width // 2, width // 4
    across_core, across_y = dp_at(1), dp_at(2)

    def core_copy(unit):
        return pltpu.make_async_remote_copy(
            src_ref=wg.at[unit_rows(unit, half_rows * (1 - core), half_rows), :],
            dst_ref=r["rc"].at[pl.ds(pl.multiple_of(unit * half_rows, 16), half_rows), :],
            send_sem=r["cs"].at[unit],
            recv_sem=r["cr"].at[unit],
            device_id=across_core,
        )

    def y_slot(unit, z_first):
        if z_first:
            at = (UNITS - Z_FIRST[1] + Z_FIRST[0]) * quarter + (unit - Z_FIRST[0]) * block
            return r["ry"].at[pl.ds(pl.multiple_of(at, 16), block), :]
        return r["ry"].at[pl.ds(pl.multiple_of(index_of(unit) * quarter, 16), quarter), :]

    def index_of(unit):
        return jnp.where(unit < Z_FIRST[0], unit, unit - (Z_FIRST[1] - Z_FIRST[0]))

    def y_copy(unit, z_first):
        if z_first:
            size, away = block, half_rows * core + 2 * block * z_at + block * (1 - y_at)
        else:
            size, away = quarter, half_rows * core + quarter * (1 - y_at)
        return pltpu.make_async_remote_copy(
            src_ref=wg.at[unit_rows(unit, away, size), :],
            dst_ref=y_slot(unit, z_first),
            send_sem=r["ys"].at[unit],
            recv_sem=r["yr"].at[unit],
            device_id=across_y,
        )

    def z_rows(unit, owner, z_first):
        if z_first:
            return unit_rows(unit, half_rows * core + 2 * block * owner, 2 * block)
        return unit_rows(unit, half_rows * core + quarter * y_at + block * owner, block)

    def z_slot(unit, slot, z_first):
        if z_first:
            at = (unit - Z_FIRST[0]) * 10 * block + slot * 2 * block
            return r["zf"].at[pl.ds(pl.multiple_of(at, 16), 2 * block), :]
        at = index_of(unit) * 5 * block + slot * block
        return r["zb"].at[pl.ds(pl.multiple_of(at, 16), block), :]

    def z_copy(unit, owner, toward, z_first, goes_to):
        up = toward > 0
        slot = owner if up or owner != goes_to else 4
        return pltpu.make_async_remote_copy(
            src_ref=wg.at[z_rows(unit, owner, z_first), :],
            dst_ref=z_slot(unit, slot, z_first),
            send_sem=r["rs" if up else "ls"].at[unit * 4 + owner],
            recv_sem=r["rr" if up else "lr"].at[unit * 4 + owner],
            device_id={"dp": lax.rem(me + n + 4 * toward, n), "section": sec},
        )

    def add_rows(unit, offset, source, size):
        for part in range(size // block):
            rows = unit_rows(unit, offset + block * part, block)
            came = source[block * part : block * (part + 1), :]
            wg[rows, :] = (wg[rows, :].astype(F32) + came.astype(F32)).astype(BF)

    def add_core(unit, z_first):
        core_copy(unit).wait_recv()
        came = r["rc"].at[pl.ds(pl.multiple_of(unit * half_rows, 16), half_rows), :]
        add_rows(unit, half_rows * core, came, half_rows)
        if z_first:
            z_start(unit, True)
        else:
            y_copy(unit, False).start()

    def z_start(unit, z_first):
        @pl.when(z_at == 0)
        def _():
            for owner in (3, 2, 1):
                z_copy(unit, owner, 1, z_first, 1).start()

        @pl.when(z_at == 3)
        def _():
            for owner in (0, 1, 2):
                z_copy(unit, owner, -1, z_first, 2).start()

    def z_hop(hop, unit, z_first):
        size = 2 * block if z_first else block

        def pass_on(here, owner, toward):
            z_copy(unit, owner, toward, z_first, here).wait_recv()
            rows = z_rows(unit, owner, z_first)
            came = z_slot(unit, owner, z_first)
            wg[rows, :] = (wg[rows, :].astype(F32) + came[...].astype(F32)).astype(BF)
            z_copy(unit, owner, toward, z_first, here + toward).start()

        def finish(here):
            total = wg[z_rows(unit, here, z_first), :].astype(F32)
            if here > 0:
                z_copy(unit, here, 1, z_first, here).wait_recv()
                total = total + z_slot(unit, here, z_first)[...].astype(F32)
            if here < 3:
                z_copy(unit, here, -1, z_first, here).wait_recv()
                total = total + z_slot(unit, 4, z_first)[...].astype(F32)
            if z_first:
                wg[z_rows(unit, here, True), :] = total.astype(BF)
                y_copy(unit, True).start()
            else:
                put(unit, total)

        @pl.when(z_at == hop)
        def _():
            for owner in range(3, hop, -1):
                pass_on(hop, owner, 1)
            if hop >= 2:
                finish(hop)

        @pl.when(z_at == 3 - hop)
        def _():
            for owner in range(3 - hop):
                pass_on(3 - hop, owner, -1)
            if hop >= 2:
                finish(3 - hop)

    def put(unit, total):
        total = total * scale

        @pl.when(unit < UP)
        def _():
            r["down"][:, pl.ds(pl.multiple_of(jnp.minimum(unit, 3) * width, 128), width)] = total

        @pl.when((unit >= UP) & (unit < OUT))
        def _():
            r["up"][pl.ds(pl.multiple_of(jnp.clip(unit - UP, 0, 3) * block, 16), block), :] = total

        @pl.when(unit == OUT)
        def _():
            r["out"][...] = total

        @pl.when(unit >= QKV)
        def _():
            r["three"][pl.ds(pl.multiple_of(jnp.clip(unit - QKV, 0, 2) * block, 16), block), :] = total

    def finish_z_first(unit):
        y_copy(unit, True).wait_recv()
        mine = unit_rows(unit, half_rows * core + 2 * block * z_at + block * y_at, block)
        came = y_slot(unit, True)[...]
        put(unit, wg[mine, :].astype(F32) + came.astype(F32))

    def add_y(unit):
        y_copy(unit, False).wait_recv()
        add_rows(unit, half_rows * core + quarter * y_at, y_slot(unit, False), quarter)
        z_start(unit, False)

    def place(owner, z_first):
        core_of, y_of, z_of = lax.rem(owner, 2), lax.rem(owner // 2, 2), owner // 4
        if z_first:
            return core_of * 8 + z_of * 2 + y_of
        return core_of * 8 + y_of * 4 + z_of

    def weight_gradient(left, right, chunk, first_unit, spread, z_first=False):
        for half in range(2):
            product = dot(left(half), right, 0, 0).astype(BF)
            for b in range(8):
                at = chunk * 16 + 8 * half + b
                if spread == 1:
                    at = 8 * half + b
                if reduce_here:
                    owner, part = at // spread, lax.rem(at, spread)
                    rows = unit_rows(first_unit + part, place(owner, z_first) * block, block)
                else:
                    rows = unit_rows(first_unit, at * block, block)
                wg[rows, :] = product[block * b : block * (b + 1), :]

    def half_lanes(half):
        return pl.ds((width // 2) * half, width // 2)

    def down_gradient():
        def one(z_first):
            def body(j, carry):
                weight_gradient(
                    lambda half: r["dy"][:, half_lanes(half)], r["act"][j], j, j, 1, z_first
                )
                if reduce_here:
                    core_copy(j).start()

                    @pl.when(j > 0)
                    def _():
                        if z_first:
                            pl.when(j == Z_FIRST[0])(lambda: add_core(j - 1, False))
                            pl.when(j > Z_FIRST[0])(lambda: add_core(j - 1, True))
                        else:
                            add_core(j - 1, False)

                return carry

            return body

        lax.fori_loop(0, Z_FIRST[0], one(False), 0)
        lax.fori_loop(*Z_FIRST, one(True), 0)
        if reduce_here:
            add_core(Z_FIRST[1] - 1, True)

    def start_units(begin, end):
        if reduce_here:
            for unit in range(begin, end):
                core_copy(unit).start()

    def z_first_hops(hop):
        if reduce_here:

            def one(unit, carry):
                z_hop(hop, unit, True)
                return carry

            lax.fori_loop(*Z_FIRST, one, 0)

    def turn(step, carry):
        img = lax.rem(step, images)
        early = step < images
        back_now = early == second
        down_now = step == jnp.where(first, 2 * images - 1, images)

        @pl.when(early)
        def _():
            forward(step, img)

        @pl.when(back_now)
        def _():
            take_gradient(img)

        @pl.when(down_now)
        def _():
            down_gradient()

        @pl.when(back_now)
        def _():
            backward_mlp(img)

        @pl.when(down_now & first)
        def _():
            z_first_hops(1)

        @pl.when(back_now)
        def _():
            backward_attention(img)

        return carry

    lax.fori_loop(0, 2 * images, turn, 0)

    def up_one(c, carry):
        weight_gradient(lambda half: r["gp"][c, :, half_lanes(half)], r["a2"][...], c, UP, 4)
        return carry

    lax.fori_loop(0, 4, up_one, 0)
    start_units(UP, OUT)
    if reduce_here:
        for unit in range(UP, UP + WINDOW):
            add_core(unit, False)

    @pl.when(second)
    def _():
        z_first_hops(1)

    z_first_hops(2)
    weight_gradient(lambda half: r["n2"][:, half_lanes(half)], r["o"][...], 0, OUT, 1)
    start_units(OUT, QKV)

    def qkv_one(c, carry):
        weight_gradient(lambda half: r["qkv"][c, :, half_lanes(half)], r["a1"][...], c, QKV, 3)
        return carry

    lax.fori_loop(0, 3, qkv_one, 0)
    start_units(QKV, UNITS)
    z_first_hops(3)

    for img in range(images):
        bound_copy(img).start()

    if reduce_here:
        hops = [dp_at(1), dp_at(2), dp_at(8), dp_at(4), across]

        def small_send(t):
            return pltpu.make_async_remote_copy(
                src_ref=r["sms"].at[t],
                dst_ref=r["smr"].at[t],
                send_sem=r["ss"].at[t],
                recv_sem=r["sr"].at[t],
                device_id=hops[t],
            )

        r["sms"][0] = r["sm"][...]
        small_send(0).start()
        in_order = UNITS - (Z_FIRST[1] - Z_FIRST[0])

        def unit_at(index):
            return jnp.where(index < Z_FIRST[0], index, index + Z_FIRST[1] - Z_FIRST[0])

        def small_step(t):
            small_send(t).wait_recv()
            if t < 4:
                r["sms"][t + 1] = r["sms"][t] + r["smr"][t]
                small_send(t + 1).start()
                return
            total = r["sms"][4] * scale
            shift = lax.rem(width - block * me, width)
            turned = pltpu.roll(total, shift, 1)[:, :block]
            r["g_gains"][0] = turned[0:2]
            r["g_shifts"][0] = turned[2:4]
            r["g_qv"][0] = turned[4:6]
            r["g_out"][...] = turned[6:7]
            r["g_down"][...] = turned[11:12]
            up_row = r["sms"][4, pl.ds(7 + me // 4, 1), :] * scale
            up_shift = lax.rem(width - 4 * block * lax.rem(me, 4), width)
            spread_row = jnp.broadcast_to(up_row, (8, width))
            r["g_up"][...] = pltpu.roll(spread_row, up_shift, 1)[0:1, : 4 * block]
            token = (r["sms"][4, 12:13, :] + r["smr"][4, 12:13, :]) * scale
            r["g_token"][...] = token.reshape(width)

        def drain(k, carry):
            @pl.when(k < in_order)
            def _():
                add_y(unit_at(k))

            @pl.when((k >= Z_FIRST[0]) & (k + WINDOW < in_order))
            def _():
                add_core(unit_at(k + WINDOW), False)

            for hop in (1, 2, 3):

                @pl.when((k >= hop) & (k < in_order + hop))
                def _(hop=hop):
                    z_hop(hop, unit_at(k - hop), False)

            for t in range(5):

                @pl.when(k == t + 1)
                def _(t=t):
                    small_step(t)

            @pl.when(k == 2)
            def _():
                for unit in range(*Z_FIRST):
                    finish_z_first(unit)

            return carry

        lax.fori_loop(0, in_order + 3, drain, 0)

        def sent(z_first):
            def body(unit, carry):
                core_copy(unit).wait_send()
                y_copy(unit, z_first).wait_send()
                for here in range(4):

                    @pl.when(z_at == here)
                    def _(here=here):
                        for owner in range(4):
                            if owner > here:
                                z_copy(unit, owner, 1, z_first, here + 1).wait_send()
                            if owner < here:
                                z_copy(unit, owner, -1, z_first, here - 1).wait_send()

                return carry

            return body

        lax.fori_loop(0, Z_FIRST[0], sent(False), 0)
        lax.fori_loop(*Z_FIRST, sent(True), 0)
        lax.fori_loop(Z_FIRST[1], UNITS, sent(False), 0)
        for t in range(5):
            small_send(t).wait_send()
    else:
        r["small"][...] = r["sm"][...] * scale
        out = pltpu.make_async_copy(wg.at[pl.ds(0, UNITS * width), :], r["grads"], r["pin_sem"])
        out.start()
        out.wait()

    for img in range(images):
        bound_copy(img).wait()

        @pl.when(first)
        def _(img=img):
            forward_send(img).wait_send()

        @pl.when(second)
        def _(img=img):
            backward_send(img).wait_send()


def hand_on(count, *refs):
    given, results, held = refs[:count], refs[count : 2 * count], refs[2 * count : 3 * count]
    sems = refs[-1]
    loads = [pltpu.make_async_copy(given[i], held[i], sems.at[0, i]) for i in range(count)]
    stores = [pltpu.make_async_copy(held[i], results[i], sems.at[1, i]) for i in range(count)]
    for load in loads:
        load.start()
    for load, store in zip(loads, stores):
        load.wait()
        store.start()
    for store in stores:
        store.wait()


def on_device(n, *args):
    (patches, block_mask, mask_token, norm_gains, norm_shifts, w_qkv, qv_bias, w_out, out_bias) = args[:9]
    w_up, up_bias, w_down, down_bias, cotangent = args[9:]
    images, seq, width = patches.shape
    pad = -(-seq // 16) * 16
    rows = images * pad
    reduce_here = n == 16
    scale = 1.0 / math.sqrt(images * n * seq)
    geo = (n, images, seq, pad, width, scale)
    block = width // 16
    anywhere = pl.BlockSpec(memory_space=pl.ANY)
    vmem = pl.BlockSpec(memory_space=pltpu.VMEM)
    shapes = [(images, seq, 1, width)]
    if reduce_here:
        shapes += [(block, 4 * width), (4 * block, width), (block, width), (3 * block, width)]
        shapes += [(1, 2, block)] * 3 + [(1, block), (1, 4 * block), (1, block), (width,)]
        out_shape = [jax.ShapeDtypeStruct(shape, F32) for shape in shapes]
    else:
        out_shape = [
            jax.ShapeDtypeStruct(shapes[0], F32),
            jax.ShapeDtypeStruct((UNITS * width, width), BF),
            jax.ShapeDtypeStruct((SMALL, width), F32),
        ]
    narrow = pltpu.VMEM((rows, width), BF)
    dma = pltpu.SemaphoreType.DMA
    scratch = [
        pltpu.VMEM((16 * width, width), BF),
        narrow,
        narrow,
        narrow,
        pltpu.VMEM((3, rows, width), BF),
        narrow,
        narrow,
        narrow,
        pltpu.VMEM((4, rows, width), BF),
        pltpu.VMEM((4, rows, width), BF),
        narrow,
        narrow,
        pltpu.VMEM((images * HEADS, pad, pad), BF),
        pltpu.VMEM((rows, 3), F32),
        pltpu.VMEM((pad, width), F32),
        pltpu.VMEM((pad, width), F32),
        pltpu.VMEM((pad, width), F32),
        pltpu.VMEM((pad, width), BF),
        pltpu.VMEM((images, seq, width), BF),
        pltpu.VMEM((images, seq, 1, width), F32),
        pltpu.VMEM((SMALL, width), F32),
        pltpu.VMEM((5, SMALL, width), F32),
        pltpu.VMEM((5, SMALL, width), F32),
        dma(()),
        dma((UNITS,)),
        dma((images,)),
        dma((images,)),
        dma((images,)),
        dma((images,)),
        dma((images,)),
    ]
    if reduce_here:
        z_first = Z_FIRST[1] - Z_FIRST[0]
        scratch += [
            pltpu.VMEM((UNITS * width // 2, width), BF),
            pltpu.VMEM((((UNITS - z_first) * 4 + z_first) * block, width), BF),
            pltpu.VMEM(((UNITS - z_first) * 5 * block, width), BF),
            pltpu.VMEM((z_first * 10 * block, width), BF),
        ]
        scratch += [dma((UNITS,))] * 4 + [dma((UNITS * 4,))] * 4 + [dma((5,))] * 2
    weights = 12 * width * width
    results = pl.pallas_call(
        functools.partial(kernel, geo),
        out_shape=out_shape,
        in_specs=[anywhere] * 2 + [vmem] * 8 + [anywhere] * 4,
        out_specs=[anywhere] + ([vmem] * 11 if reduce_here else [anywhere, vmem]),
        scratch_shapes=scratch,
        compiler_params=pltpu.CompilerParams(
            collective_id=0, has_side_effects=True, vmem_limit_bytes=64 * 1024 * 1024 - 65536
        ),
        cost_estimate=pl.CostEstimate(
            flops=6 * rows * weights, bytes_accessed=4 * weights, transcendentals=rows * width * 8
        ),
        name="relay",
    )(
        patches,
        cotangent,
        block_mask,
        mask_token,
        norm_gains[0],
        norm_shifts[0],
        qv_bias[0],
        out_bias,
        up_bias,
        down_bias,
        w_qkv,
        w_out,
        w_up,
        w_down,
    )
    if reduce_here:
        count = len(out_shape)
        results = pl.pallas_call(
            functools.partial(hand_on, count),
            out_shape=out_shape,
            in_specs=[anywhere] * count,
            out_specs=[anywhere] * count,
            scratch_shapes=[pltpu.VMEM(a.shape, a.dtype) for a in out_shape] + [dma((2, count))],
            name="hand_on",
        )(*results)
        bound, down, up, out, qkv, gains, shifts, qv, out_vector, up_vector, down_vector, token = results
        boundary = bound.transpose(2, 0, 1, 3)
        parts = (boundary, token, gains, shifts, qkv.T[None], qv, out.T[None], out_vector, up.T[None])
        return (*parts, up_vector, down.reshape(block, 4 * width).T[None], down_vector)
    bound, grads, small = results
    me = lax.axis_index("dp")
    share = width // n
    token = lax.psum(small[12], ("dp", "section"))
    vectors = lax.psum(small[:12], "dp")
    wide = grads.astype(F32) * scale

    def scattered(first, count):
        part = wide[first * width : (first + count) * width]
        return lax.psum_scatter(part, "dp", scatter_dimension=0, tiled=True).T

    down = lax.psum_scatter(
        wide[: 4 * width].reshape(4, width, width), "dp", scatter_dimension=1, tiled=True
    )
    down = down.transpose(0, 2, 1).reshape(4 * width, share)
    up = scattered(UP, 4)
    out = scattered(OUT, 1)
    qkv = scattered(QKV, 3)

    def cut(first, count):
        return lax.dynamic_slice(vectors, (first, me * share), (count, share))

    up_vector = lax.dynamic_slice(vectors[7:11].reshape(-1), (me * 4 * share,), (4 * share,))
    parts = (bound.transpose(2, 0, 1, 3), token, cut(0, 2)[None], cut(2, 2)[None], qkv[None])
    parts += (cut(4, 2)[None], out[None], cut(6, 1), up[None], up_vector[None], down[None], cut(11, 1))
    return parts


def solution(mesh):
    return jax.shard_map(
        functools.partial(on_device, mesh.shape["dp"]),
        mesh=mesh,
        in_specs=(
            P("dp", None, None),
            P("dp", None),
            P(),
            P("section", None, None),
            P("section", None, None),
            P("section", None, None),
            P("section", None, None),
            P("section", None, None),
            P("section", None),
            P("section", None, None),
            P("section", None),
            P("section", None, None),
            P("section", None),
            P("dp", None, None),
        ),
        out_specs=(
            P("section", "dp", None, None),
            P(),
            P("section", None, "dp"),
            P("section", None, "dp"),
            P("section", None, "dp"),
            P("section", None, "dp"),
            P("section", None, "dp"),
            P("section", "dp"),
            P("section", None, "dp"),
            P("section", "dp"),
            P("section", None, "dp"),
            P("section", "dp"),
        ),
        check_vma=False,
    )
```

```python
import functools
import math

import jax
import jax.numpy as jnp
from jax import lax
from jax.experimental import pallas as pl
from jax.experimental.pallas import tpu as pltpu
from jax.sharding import PartitionSpec as P

HEADS = 12
EPS = 1e-06
BF = jnp.bfloat16
F32 = jnp.float32
Z_FIRST = (3, 5)
WINDOW = 4
UNITS = 12
UP, OUT, QKV, DOWN_W = 4, 8, 9, 12
SMALL = 16
INV_SQRT2 = 1.0 / math.sqrt(2.0)
INV_SQRT2PI = 1.0 / math.sqrt(2.0 * math.pi)


def dot(a, b, contract_a, contract_b):
    return lax.dot_general(
        a, b, (((contract_a,), (contract_b,)), ((), ())), preferred_element_type=F32
    )


def fold8(x):
    rows, width = x.shape
    return jnp.sum(x.reshape(rows // 8, 8, width), axis=0)


def kernel(geo, *refs):
    (n, images, seq, pad, width, scale) = geo
    reduce_here = n == 16
    total_rows = images * pad
    block = width // 16
    names = ["patches", "cotangent", "mask", "token", "gains", "shifts", "qv_bias", "out_bias", "up_bias"]
    names += ["down_bias", "w_qkv", "w_out", "w_up", "w_down", "bound"]
    if reduce_here:
        names += ["down", "up", "out", "three", "g_gains", "g_shifts", "g_qv", "g_out", "g_up", "g_down"]
        names += ["g_token"]
    else:
        names += ["grads", "small"]
    names += ["wg", "x", "n1", "a1", "qkv", "o", "n2", "a2", "act", "gp", "dy", "send", "prob", "cols"]
    names += ["yb", "da", "tb", "do", "pin", "plain", "sm", "sms", "smr"]
    names += ["pin_sem", "w_sem", "out_sem", "fs", "fr", "bs", "br"]
    if reduce_here:
        names += ["rc", "ry", "zb", "zf", "cs", "cr", "ys", "yr", "rs", "rr", "ls", "lr", "ss", "sr"]
    r = dict(zip(names, refs, strict=True))
    wg = r["wg"]
    me = lax.axis_index("dp")
    sec = lax.axis_index("section")
    first, second = sec == 0, sec == 1

    def dp_at(bit):
        mine = lax.rem(me // bit, 2)
        return {"dp": me + bit - 2 * bit * mine, "section": sec}

    across = {"dp": me, "section": 1 - sec}
    core, y_at, z_at = lax.rem(me, 2), lax.rem(me // 2, 2), me // 4
    partners = [across]
    if reduce_here:
        partners += [dp_at(1), dp_at(2)]
        partners += [{"dp": lax.rem(me + 4 * turn, n), "section": sec} for turn in (1, 2, 3)]

    def unit_rows(unit, offset=0, size=width):
        return pl.ds(pl.multiple_of(unit * width + offset, 16), size)

    weight_copies = []
    for j in range(3):
        weight_copies.append((QKV + j, r["w_qkv"].at[0, :, pl.ds(width * j, width)]))
    weight_copies.append((OUT, r["w_out"].at[0]))
    for j in range(4):
        weight_copies.append((UP + j, r["w_up"].at[0, :, pl.ds(width * j, width)]))
    for j in range(4):
        weight_copies.append((DOWN_W + j, r["w_down"].at[0, pl.ds(width * j, width), :]))

    def weight_copy(index):
        unit, source = weight_copies[index]
        return pltpu.make_async_copy(source, wg.at[unit_rows(unit), :], r["w_sem"].at[index])

    @pl.when(first)
    def _():
        pltpu.make_async_copy(r["patches"], r["pin"], r["pin_sem"]).start()

    @pl.when(second)
    def _():
        pltpu.make_async_copy(r["cotangent"], r["pin"], r["pin_sem"]).start()

    for index in range(3):
        weight_copy(index).start()

    barrier = pltpu.get_barrier_semaphore()
    for partner in partners:
        pl.semaphore_signal(barrier, inc=1, device_id=partner)

    r["sm"][...] = jnp.zeros_like(r["sm"])
    pltpu.make_async_copy(r["patches"], r["pin"], r["pin_sem"]).wait()

    def image_rows(img, offset=0, size=pad):
        return pl.ds(pl.multiple_of(img * pad + offset, 16), size)

    def forward_send(img):
        rows = image_rows(img)
        return pltpu.make_async_remote_copy(
            src_ref=r["send"].at[rows, :],
            dst_ref=r["x"].at[rows, :],
            send_sem=r["fs"].at[img],
            recv_sem=r["fr"].at[img],
            device_id=across,
        )

    def backward_send(img):
        rows = image_rows(img)
        return pltpu.make_async_remote_copy(
            src_ref=r["send"].at[rows, :],
            dst_ref=r["dy"].at[rows, :],
            send_sem=r["bs"].at[img],
            recv_sem=r["br"].at[img],
            device_id=across,
        )

    def bound_copy(img):
        return pltpu.make_async_copy(r["plain"].at[img], r["bound"].at[img], r["out_sem"].at[img])

    def write_bound(img, at, values):
        size = min(16, seq - at)
        r["plain"][img, at : at + size, 0, :] = values[:size]

    def row_blocks(img):
        return [image_rows(img, 16 * b, 16) for b in range(pad // 16)]

    def norm_forward(img, read, which, normed, scaled):
        gain = r["gains"][which : which + 1, :]
        shift = r["shifts"][which : which + 1, :]
        for b, rows in enumerate(row_blocks(img)):
            values = read(b, rows)
            centered = values - jnp.mean(values, axis=1, keepdims=True)
            variance = jnp.mean(centered * centered, axis=1, keepdims=True)
            inverse = lax.rsqrt(variance + EPS)
            unit = centered * inverse
            r["cols"][rows, which : which + 1] = inverse
            normed[rows, :] = unit.astype(BF)
            scaled[rows, :] = (unit * gain + shift).astype(BF)

    def halves(values):
        lane = lax.broadcasted_iota(jnp.int32, values.shape, 1)
        zero = jnp.zeros_like(values)
        low = lane < width // HEADS
        return jnp.where(low, values, zero), jnp.where(low, zero, values)

    def attention_forward(img, pair):
        rows = image_rows(img)
        lanes = pl.ds(128 * pair, 128)
        queries = r["qkv"][0, rows, lanes]
        keys = r["qkv"][1, rows, lanes]
        values = r["qkv"][2, rows, lanes]
        mixed = []
        for head, part in enumerate(halves(queries)):
            scores = dot(keys, part, 1, 1)
            key_at = lax.broadcasted_iota(jnp.int32, scores.shape, 0)
            scores = jnp.where(key_at < seq, scores, -1e30)
            raised = jnp.exp(scores - jnp.max(scores, axis=0, keepdims=True))
            share = 1.0 / jnp.sum(raised, axis=0, keepdims=True)
            prob = (raised * share).astype(BF)
            r["prob"][img * HEADS + 2 * pair + head] = prob
            mixed.append(dot(prob, values, 0, 0))
        lane = lax.broadcasted_iota(jnp.int32, mixed[0].shape, 1)
        r["o"][rows, lanes] = jnp.where(lane < width // HEADS, mixed[0], mixed[1]).astype(BF)

    def wait_weights(step, indices, then_start=()):
        @pl.when(step == 0)
        def _():
            for index in indices:
                weight_copy(index).wait()
            for index in then_start:
                weight_copy(index).start()

    def forward(step, img):
        rows = image_rows(img)

        @pl.when(first)
        def _():
            tail = image_rows(img, seq // 16 * 16, 16)
            r["x"][tail, :] = jnp.zeros((16, width), BF)
            row = r["mask"][pl.ds(img, 1), :]
            at_row = lax.broadcasted_iota(jnp.int32, (pad, seq), 0)
            at_lane = lax.broadcasted_iota(jnp.int32, (pad, seq), 1)
            covered = jnp.where((at_row == at_lane) & (row == 1), 1.0, 0.0)
            column = jnp.sum(covered, axis=1, keepdims=True)
            r["cols"][rows, 2:3] = column
            token = r["token"][...][None, :].astype(F32)
            kept = r["pin"][img].astype(F32)
            mixed = jnp.where(column[:seq] > 0.5, token, kept)
            r["x"][image_rows(img, 0, seq), :] = mixed.astype(BF)

        @pl.when(second)
        def _():
            forward_send(img).wait_recv()

        norm_forward(img, lambda b, at: r["x"][at, :].astype(F32), 0, r["n1"], r["a1"])
        wait_weights(step, range(0, 3), range(3, UNITS))
        for j in range(3):
            projected = dot(r["a1"][rows, :], wg[unit_rows(QKV + j), :], 1, 0)
            if j == 0:
                projected = (projected + r["qv_bias"][0:1, :]) * (1.0 / math.sqrt(width // HEADS))
            if j == 2:
                projected = projected + r["qv_bias"][1:2, :]
            r["qkv"][j, rows, :] = projected.astype(BF)

        for pair in range(HEADS // 2):
            attention_forward(img, pair)
        wait_weights(step, range(3, 4))
        r["yb"][...] = (
            r["x"][rows, :].astype(F32)
            + dot(r["o"][rows, :], wg[unit_rows(OUT), :], 1, 0)
            + r["out_bias"][...]
        )
        norm_forward(img, lambda b, at: r["yb"][16 * b : 16 * (b + 1), :], 1, r["n2"], r["a2"])
        wait_weights(step, range(4, UNITS))
        result = None
        for j in range(4):
            hidden = dot(r["a2"][rows, :], wg[unit_rows(UP + j), :], 1, 0)
            hidden = hidden + r["up_bias"][:, width * j : width * (j + 1)]
            below = 0.5 + 0.5 * lax.erf(hidden * INV_SQRT2)
            slope = below + hidden * (jnp.exp(hidden * hidden * -0.5) * INV_SQRT2PI)
            active = (hidden * below).astype(BF)
            r["act"][j, rows, :] = active
            r["gp"][j, rows, :] = slope.astype(BF)
            term = dot(active, wg[unit_rows(DOWN_W + j), :], 1, 0)
            result = term if result is None else result + term
        result = r["yb"][...] + result + r["down_bias"][...]

        @pl.when(step == 0)
        def _():
            pl.semaphore_wait(barrier, len(partners))

        @pl.when(first)
        def _():
            r["send"][rows, :] = result.astype(BF)
            forward_send(img).start()

        @pl.when(second)
        def _():
            for at in range(0, seq, 16):
                write_bound(img, at, result[at : at + 16])

    def take_gradient(img):
        @pl.when(first)
        def _():
            backward_send(img).wait_recv()

        @pl.when(second)
        def _():
            tail = image_rows(img, seq // 16 * 16, 16)
            r["dy"][tail, :] = jnp.zeros((16, width), BF)
            r["dy"][image_rows(img, 0, seq), :] = r["pin"][img]

    def norm_backward(img, which, gradient, incoming):
        results = []
        gain = r["gains"][which : which + 1, :]
        normed = r["n1"] if which == 0 else r["n2"]
        gain_sum = jnp.zeros((8, width), F32)
        shift_sum = jnp.zeros((8, width), F32)
        for b, rows in enumerate(row_blocks(img)):
            here = gradient[16 * b : 16 * (b + 1), :]
            unit = normed[rows, :].astype(F32)
            gain_sum = gain_sum + fold8(here * unit)
            shift_sum = shift_sum + fold8(here)
            scaled = here * gain
            mean = jnp.mean(scaled, axis=1, keepdims=True)
            along = jnp.mean(scaled * unit, axis=1, keepdims=True)
            local = (scaled - mean - unit * along) * r["cols"][rows, which : which + 1]
            results.append((b, rows, local + incoming(b, rows)))
        r["sm"][which : which + 1, :] += jnp.sum(gain_sum, axis=0, keepdims=True)
        r["sm"][2 + which : 3 + which, :] += jnp.sum(shift_sum, axis=0, keepdims=True)
        return results

    def backward_mlp(img):
        rows = image_rows(img)
        incoming = r["dy"][rows, :]
        r["sm"][11:12, :] += jnp.sum(incoming.astype(F32), axis=0, keepdims=True)
        back = None
        for j in range(4):
            change = dot(incoming, wg[unit_rows(DOWN_W + j), :], 1, 1)
            change = change * r["gp"][j, rows, :].astype(F32)
            r["sm"][7 + j : 8 + j, :] += jnp.sum(change, axis=0, keepdims=True)
            narrow = change.astype(BF)
            r["gp"][j, rows, :] = narrow
            term = dot(narrow, wg[unit_rows(UP + j), :], 1, 1)
            back = term if back is None else back + term
        r["tb"][...] = back
        bias_sum = jnp.zeros((8, width), F32)
        for b, block_rows, middle in norm_backward(
            img, 1, r["tb"], lambda b, block_rows: r["dy"][block_rows, :].astype(F32)
        ):
            bias_sum = bias_sum + fold8(middle)
            r["da"][16 * b : 16 * (b + 1), :] = middle
            r["n2"][block_rows, :] = middle.astype(BF)
        r["sm"][6:7, :] += jnp.sum(bias_sum, axis=0, keepdims=True)

    def attention_backward(img, pairs):
        rows = image_rows(img)
        places = [pl.ds(128 * pair, 128) for pair in pairs]
        loaded = []
        for pair, lanes in zip(pairs, places):
            probs = [r["prob"][img * HEADS + 2 * pair + head] for head in range(2)]
            loaded.append((*[r["qkv"][i, rows, lanes] for i in range(3)], r["do"][:, lanes], probs))
        results = []
        for queries, keys, values, back, probs in loaded:
            query_parts, key_parts, back_parts = halves(queries), halves(keys), halves(back)
            total = None
            for head in range(2):
                wide = probs[head].astype(F32)
                change = dot(values, back_parts[head], 1, 1)
                carried = jnp.sum(wide * change, axis=0, keepdims=True)
                scores = (wide * (change - carried)).astype(BF)
                terms = (
                    dot(scores, key_parts[head], 0, 0),
                    dot(scores, query_parts[head], 1, 0),
                    dot(probs[head], back_parts[head], 1, 0),
                )
                total = terms if total is None else [a + b for a, b in zip(total, terms)]
            d_query, d_key, d_value = total
            results.append((d_query * (1.0 / math.sqrt(width // HEADS)), d_key, d_value))
        for (d_query, d_key, d_value), lanes in zip(results, places):
            r["sm"][4:5, lanes] += jnp.sum(d_query, axis=0, keepdims=True)
            r["sm"][5:6, lanes] += jnp.sum(d_value, axis=0, keepdims=True)
            r["qkv"][0, rows, lanes] = d_query.astype(BF)
            r["qkv"][1, rows, lanes] = d_key.astype(BF)
            r["qkv"][2, rows, lanes] = d_value.astype(BF)

    def backward_attention(img):
        rows = image_rows(img)
        r["do"][...] = dot(r["n2"][rows, :], wg[unit_rows(OUT), :], 1, 1).astype(BF)

        attention_backward(img, range(HEADS // 2))
        back = None
        for j in range(3):
            term = dot(r["qkv"][j, rows, :], wg[unit_rows(QKV + j), :], 1, 1)
            back = term if back is None else back + term
        r["tb"][...] = back
        for b, block_rows, entry in norm_backward(
            img, 0, r["tb"], lambda b, block_rows: r["da"][16 * b : 16 * (b + 1), :]
        ):
            r["da"][16 * b : 16 * (b + 1), :] = entry

        @pl.when(first)
        def _():
            token_sum = jnp.zeros((8, width), F32)
            for b, block_rows in enumerate(row_blocks(img)):
                entry = r["da"][16 * b : 16 * (b + 1), :]
                under = r["cols"][block_rows, 2:3] > 0.5
                token_sum = token_sum + fold8(jnp.where(under, entry, 0.0))
                if 16 * b < seq:
                    write_bound(img, 16 * b, jnp.where(under, 0.0, entry))
            r["sm"][12:13, :] += jnp.sum(token_sum, axis=0, keepdims=True)

        @pl.when(second)
        def _():
            r["send"][rows, :] = r["da"][...].astype(BF)
            backward_send(img).start()

    half_rows, quarter = width // 2, width // 4
    across_core, across_y = dp_at(1), dp_at(2)

    def core_copy(unit):
        return pltpu.make_async_remote_copy(
            src_ref=wg.at[unit_rows(unit, half_rows * (1 - core), half_rows), :],
            dst_ref=r["rc"].at[pl.ds(pl.multiple_of(unit * half_rows, 16), half_rows), :],
            send_sem=r["cs"].at[unit],
            recv_sem=r["cr"].at[unit],
            device_id=across_core,
        )

    def y_slot(unit, z_first):
        if z_first:
            at = (UNITS - Z_FIRST[1] + Z_FIRST[0]) * quarter + (unit - Z_FIRST[0]) * block
            return r["ry"].at[pl.ds(pl.multiple_of(at, 16), block), :]
        return r["ry"].at[pl.ds(pl.multiple_of(index_of(unit) * quarter, 16), quarter), :]

    def index_of(unit):
        return jnp.where(unit < Z_FIRST[0], unit, unit - (Z_FIRST[1] - Z_FIRST[0]))

    def y_copy(unit, z_first):
        if z_first:
            size, away = block, half_rows * core + 2 * block * z_at + block * (1 - y_at)
        else:
            size, away = quarter, half_rows * core + quarter * (1 - y_at)
        return pltpu.make_async_remote_copy(
            src_ref=wg.at[unit_rows(unit, away, size), :],
            dst_ref=y_slot(unit, z_first),
            send_sem=r["ys"].at[unit],
            recv_sem=r["yr"].at[unit],
            device_id=across_y,
        )

    def z_rows(unit, owner, z_first):
        if z_first:
            return unit_rows(unit, half_rows * core + 2 * block * owner, 2 * block)
        return unit_rows(unit, half_rows * core + quarter * y_at + block * owner, block)

    def z_slot(unit, slot, z_first):
        if z_first:
            at = (unit - Z_FIRST[0]) * 10 * block + slot * 2 * block
            return r["zf"].at[pl.ds(pl.multiple_of(at, 16), 2 * block), :]
        at = index_of(unit) * 5 * block + slot * block
        return r["zb"].at[pl.ds(pl.multiple_of(at, 16), block), :]

    def z_copy(unit, owner, toward, z_first, goes_to):
        up = toward > 0
        slot = owner if up or owner != goes_to else 4
        return pltpu.make_async_remote_copy(
            src_ref=wg.at[z_rows(unit, owner, z_first), :],
            dst_ref=z_slot(unit, slot, z_first),
            send_sem=r["rs" if up else "ls"].at[unit * 4 + owner],
            recv_sem=r["rr" if up else "lr"].at[unit * 4 + owner],
            device_id={"dp": lax.rem(me + n + 4 * toward, n), "section": sec},
        )

    def add_rows(unit, offset, source, size):
        for part in range(size // block):
            rows = unit_rows(unit, offset + block * part, block)
            came = source[block * part : block * (part + 1), :]
            wg[rows, :] = (wg[rows, :].astype(F32) + came.astype(F32)).astype(BF)

    def add_core(unit, z_first):
        core_copy(unit).wait_recv()
        came = r["rc"].at[pl.ds(pl.multiple_of(unit * half_rows, 16), half_rows), :]
        add_rows(unit, half_rows * core, came, half_rows)
        if z_first:
            z_start(unit, True)
        else:
            y_copy(unit, False).start()

    def z_start(unit, z_first):
        @pl.when(z_at == 0)
        def _():
            for owner in (3, 2, 1):
                z_copy(unit, owner, 1, z_first, 1).start()

        @pl.when(z_at == 3)
        def _():
            for owner in (0, 1, 2):
                z_copy(unit, owner, -1, z_first, 2).start()

    def z_hop(hop, unit, z_first):
        size = 2 * block if z_first else block

        def pass_on(here, owner, toward):
            z_copy(unit, owner, toward, z_first, here).wait_recv()
            rows = z_rows(unit, owner, z_first)
            came = z_slot(unit, owner, z_first)
            wg[rows, :] = (wg[rows, :].astype(F32) + came[...].astype(F32)).astype(BF)
            z_copy(unit, owner, toward, z_first, here + toward).start()

        def finish(here):
            total = wg[z_rows(unit, here, z_first), :].astype(F32)
            if here > 0:
                z_copy(unit, here, 1, z_first, here).wait_recv()
                total = total + z_slot(unit, here, z_first)[...].astype(F32)
            if here < 3:
                z_copy(unit, here, -1, z_first, here).wait_recv()
                total = total + z_slot(unit, 4, z_first)[...].astype(F32)
            if z_first:
                wg[z_rows(unit, here, True), :] = total.astype(BF)
                y_copy(unit, True).start()
            else:
                put(unit, total)

        @pl.when(z_at == hop)
        def _():
            for owner in range(3, hop, -1):
                pass_on(hop, owner, 1)
            if hop >= 2:
                finish(hop)

        @pl.when(z_at == 3 - hop)
        def _():
            for owner in range(3 - hop):
                pass_on(3 - hop, owner, -1)
            if hop >= 2:
                finish(3 - hop)

    def put(unit, total):
        total = total * scale

        @pl.when(unit < UP)
        def _():
            r["down"][:, pl.ds(pl.multiple_of(jnp.minimum(unit, 3) * width, 128), width)] = total

        @pl.when((unit >= UP) & (unit < OUT))
        def _():
            r["up"][pl.ds(pl.multiple_of(jnp.clip(unit - UP, 0, 3) * block, 16), block), :] = total

        @pl.when(unit == OUT)
        def _():
            r["out"][...] = total

        @pl.when(unit >= QKV)
        def _():
            r["three"][pl.ds(pl.multiple_of(jnp.clip(unit - QKV, 0, 2) * block, 16), block), :] = total

    def finish_z_first(unit):
        y_copy(unit, True).wait_recv()
        mine = unit_rows(unit, half_rows * core + 2 * block * z_at + block * y_at, block)
        came = y_slot(unit, True)[...]
        put(unit, wg[mine, :].astype(F32) + came.astype(F32))

    def add_y(unit):
        y_copy(unit, False).wait_recv()
        add_rows(unit, half_rows * core + quarter * y_at, y_slot(unit, False), quarter)
        z_start(unit, False)

    def place(owner, z_first):
        core_of, y_of, z_of = lax.rem(owner, 2), lax.rem(owner // 2, 2), owner // 4
        if z_first:
            return core_of * 8 + z_of * 2 + y_of
        return core_of * 8 + y_of * 4 + z_of

    def weight_gradient(left, right, chunk, first_unit, spread, z_first=False):
        for half in range(2):
            product = dot(left(half), right, 0, 0).astype(BF)
            for b in range(8):
                at = chunk * 16 + 8 * half + b
                if spread == 1:
                    at = 8 * half + b
                if reduce_here:
                    owner, part = at // spread, lax.rem(at, spread)
                    if spread == 4:
                        part = b % spread
                        z_first = UP + part < Z_FIRST[1]
                    rows = unit_rows(first_unit + part, place(owner, z_first) * block, block)
                else:
                    rows = unit_rows(first_unit, at * block, block)
                wg[rows, :] = product[block * b : block * (b + 1), :]

    def half_lanes(half):
        return pl.ds((width // 2) * half, width // 2)

    def down_gradient():
        def one(z_first):
            def body(j, carry):
                weight_gradient(
                    lambda half: r["dy"][:, half_lanes(half)], r["act"][j], j, j, 1, z_first
                )
                if reduce_here:
                    core_copy(j).start()
                    pl.when(j > 0)(lambda: add_core(j - 1, False))
                return carry

            return body

        lax.fori_loop(0, Z_FIRST[0], one(False), 0)
        lax.fori_loop(Z_FIRST[0], 4, one(True), 0)
        if reduce_here:
            add_core(3, True)

    def start_units(begin, end):
        if reduce_here:
            for unit in range(begin, end):
                core_copy(unit).start()

    def add_y_if(when, unit):
        if reduce_here:
            pl.when(when)(lambda: add_y(unit))

    def turn(step, carry):
        img = lax.rem(step, images)
        early = step < images
        back_now = early == second
        down_now = step == jnp.where(first, 2 * images - 1, images)

        @pl.when(early)
        def _():
            forward(step, img)

        @pl.when(back_now)
        def _():
            take_gradient(img)

        @pl.when(down_now)
        def _():
            down_gradient()

        @pl.when(back_now)
        def _():
            backward_mlp(img)

        add_y_if(down_now & first, 0)

        @pl.when(back_now)
        def _():
            backward_attention(img)

        return carry

    lax.fori_loop(0, 2 * images, turn, 0)

    def up_one(c, carry):
        weight_gradient(lambda half: r["gp"][c, :, half_lanes(half)], r["a2"][...], c, UP, 4)
        return carry

    lax.fori_loop(0, 4, up_one, 0)
    start_units(UP, OUT)
    if reduce_here:
        add_core(UP, True)
        for unit in range(Z_FIRST[1], OUT):
            add_core(unit, False)
    add_y_if(first, 1)
    add_y_if(second, 0)
    weight_gradient(lambda half: r["n2"][:, half_lanes(half)], r["o"][...], 0, OUT, 1)
    start_units(OUT, QKV)

    def qkv_one(c, carry):
        weight_gradient(lambda half: r["qkv"][c, :, half_lanes(half)], r["a1"][...], c, QKV, 3)
        return carry

    lax.fori_loop(0, 3, qkv_one, 0)
    start_units(QKV, UNITS)

    for img in range(images):
        bound_copy(img).start()

    if reduce_here:
        hops = [dp_at(1), dp_at(2), dp_at(8), dp_at(4), across]

        def small_send(t):
            return pltpu.make_async_remote_copy(
                src_ref=r["sms"].at[t],
                dst_ref=r["smr"].at[t],
                send_sem=r["ss"].at[t],
                recv_sem=r["sr"].at[t],
                device_id=hops[t],
            )

        r["sms"][0] = r["sm"][...]
        small_send(0).start()
        in_order = UNITS - (Z_FIRST[1] - Z_FIRST[0])

        def unit_at(index):
            return jnp.where(index < Z_FIRST[0], index, index + Z_FIRST[1] - Z_FIRST[0])

        def small_step(t):
            small_send(t).wait_recv()
            if t < 4:
                r["sms"][t + 1] = r["sms"][t] + r["smr"][t]
                small_send(t + 1).start()
                return
            total = r["sms"][4] * scale
            shift = lax.rem(width - block * me, width)
            turned = pltpu.roll(total, shift, 1)[:, :block]
            r["g_gains"][0] = turned[0:2]
            r["g_shifts"][0] = turned[2:4]
            r["g_qv"][0] = turned[4:6]
            r["g_out"][...] = turned[6:7]
            r["g_down"][...] = turned[11:12]
            up_row = r["sms"][4, pl.ds(7 + me // 4, 1), :] * scale
            up_shift = lax.rem(width - 4 * block * lax.rem(me, 4), width)
            spread_row = jnp.broadcast_to(up_row, (8, width))
            r["g_up"][...] = pltpu.roll(spread_row, up_shift, 1)[0:1, : 4 * block]
            token = (r["sms"][4, 12:13, :] + r["smr"][4, 12:13, :]) * scale
            r["g_token"][...] = token.reshape(width)

        def drain(k, carry):
            @pl.when((k < in_order) & ((k > 1) | second))
            def _():
                add_y(unit_at(k))

            @pl.when((k > 1) & (k + WINDOW < in_order))
            def _():
                add_core(unit_at(k + WINDOW), False)

            for hop in (1, 2, 3):

                @pl.when((k >= hop) & (k < hop + Z_FIRST[1] - Z_FIRST[0]))
                def _(hop=hop):
                    z_hop(hop, Z_FIRST[0] + k - hop, True)

            for hop in (1, 2, 3):

                @pl.when((k >= hop) & (k < in_order + hop))
                def _(hop=hop):
                    z_hop(hop, unit_at(k - hop), False)

            for t in range(5):

                @pl.when(k == t + 1)
                def _(t=t):
                    small_step(t)

            @pl.when((k >= 5) & (k < 5 + Z_FIRST[1] - Z_FIRST[0]))
            def _():
                finish_z_first(Z_FIRST[0] + k - 5)

            return carry

        lax.fori_loop(1, in_order + 3, drain, 0)

        def sent(z_first):
            def body(unit, carry):
                core_copy(unit).wait_send()
                y_copy(unit, z_first).wait_send()
                for here in range(4):

                    @pl.when(z_at == here)
                    def _(here=here):
                        for owner in range(4):
                            if owner > here:
                                z_copy(unit, owner, 1, z_first, here + 1).wait_send()
                            if owner < here:
                                z_copy(unit, owner, -1, z_first, here - 1).wait_send()

                return carry

            return body

        lax.fori_loop(0, Z_FIRST[0], sent(False), 0)
        lax.fori_loop(*Z_FIRST, sent(True), 0)
        lax.fori_loop(Z_FIRST[1], UNITS, sent(False), 0)
        for t in range(5):
            small_send(t).wait_send()
    else:
        r["small"][...] = r["sm"][...] * scale
        out = pltpu.make_async_copy(wg.at[pl.ds(0, UNITS * width), :], r["grads"], r["pin_sem"])
        out.start()
        out.wait()

    for img in range(images):
        bound_copy(img).wait()

        @pl.when(first)
        def _(img=img):
            forward_send(img).wait_send()

        @pl.when(second)
        def _(img=img):
            backward_send(img).wait_send()


def hand_on(count, *refs):
    given, results, held = refs[:count], refs[count : 2 * count], refs[2 * count : 3 * count]
    sems = refs[-1]
    loads = [pltpu.make_async_copy(given[i], held[i], sems.at[0, i]) for i in range(count)]
    stores = [pltpu.make_async_copy(held[i], results[i], sems.at[1, i]) for i in range(count)]
    for load in loads:
        load.start()
    for load, store in zip(loads, stores):
        load.wait()
        store.start()
    for store in stores:
        store.wait()


def on_device(n, *args):
    (patches, block_mask, mask_token, norm_gains, norm_shifts, w_qkv, qv_bias, w_out, out_bias) = args[:9]
    w_up, up_bias, w_down, down_bias, cotangent = args[9:]
    images, seq, width = patches.shape
    pad = -(-seq // 16) * 16
    rows = images * pad
    reduce_here = n == 16
    scale = 1.0 / math.sqrt(images * n * seq)
    geo = (n, images, seq, pad, width, scale)
    block = width // 16
    anywhere = pl.BlockSpec(memory_space=pl.ANY)
    vmem = pl.BlockSpec(memory_space=pltpu.VMEM)
    shapes = [(images, seq, 1, width)]
    if reduce_here:
        shapes += [(block, 4 * width), (4 * block, width), (block, width), (3 * block, width)]
        shapes += [(1, 2, block)] * 3 + [(1, block), (1, 4 * block), (1, block), (width,)]
        out_shape = [jax.ShapeDtypeStruct(shape, F32) for shape in shapes]
    else:
        out_shape = [
            jax.ShapeDtypeStruct(shapes[0], F32),
            jax.ShapeDtypeStruct((UNITS * width, width), BF),
            jax.ShapeDtypeStruct((SMALL, width), F32),
        ]
    narrow = pltpu.VMEM((rows, width), BF)
    dma = pltpu.SemaphoreType.DMA
    scratch = [
        pltpu.VMEM((16 * width, width), BF),
        narrow,
        narrow,
        narrow,
        pltpu.VMEM((3, rows, width), BF),
        narrow,
        narrow,
        narrow,
        pltpu.VMEM((4, rows, width), BF),
        pltpu.VMEM((4, rows, width), BF),
        narrow,
        narrow,
        pltpu.VMEM((images * HEADS, pad, pad), BF),
        pltpu.VMEM((rows, 3), F32),
        pltpu.VMEM((pad, width), F32),
        pltpu.VMEM((pad, width), F32),
        pltpu.VMEM((pad, width), F32),
        pltpu.VMEM((pad, width), BF),
        pltpu.VMEM((images, seq, width), BF),
        pltpu.VMEM((images, seq, 1, width), F32),
        pltpu.VMEM((SMALL, width), F32),
        pltpu.VMEM((5, SMALL, width), F32),
        pltpu.VMEM((5, SMALL, width), F32),
        dma(()),
        dma((UNITS,)),
        dma((images,)),
        dma((images,)),
        dma((images,)),
        dma((images,)),
        dma((images,)),
    ]
    if reduce_here:
        z_first = Z_FIRST[1] - Z_FIRST[0]
        scratch += [
            pltpu.VMEM((UNITS * width // 2, width), BF),
            pltpu.VMEM((((UNITS - z_first) * 4 + z_first) * block, width), BF),
            pltpu.VMEM(((UNITS - z_first) * 5 * block, width), BF),
            pltpu.VMEM((z_first * 10 * block, width), BF),
        ]
        scratch += [dma((UNITS,))] * 4 + [dma((UNITS * 4,))] * 4 + [dma((5,))] * 2
    weights = 12 * width * width
    results = pl.pallas_call(
        functools.partial(kernel, geo),
        out_shape=out_shape,
        in_specs=[anywhere] * 2 + [vmem] * 8 + [anywhere] * 4,
        out_specs=[anywhere] + ([vmem] * 11 if reduce_here else [anywhere, vmem]),
        scratch_shapes=scratch,
        compiler_params=pltpu.CompilerParams(
            collective_id=0, has_side_effects=True, vmem_limit_bytes=64 * 1024 * 1024 - 65536
        ),
        cost_estimate=pl.CostEstimate(
            flops=6 * rows * weights, bytes_accessed=4 * weights, transcendentals=rows * width * 8
        ),
        name="relay",
    )(
        patches,
        cotangent,
        block_mask,
        mask_token,
        norm_gains[0],
        norm_shifts[0],
        qv_bias[0],
        out_bias,
        up_bias,
        down_bias,
        w_qkv,
        w_out,
        w_up,
        w_down,
    )
    if reduce_here:
        count = len(out_shape)
        results = pl.pallas_call(
            functools.partial(hand_on, count),
            out_shape=out_shape,
            in_specs=[anywhere] * count,
            out_specs=[anywhere] * count,
            scratch_shapes=[pltpu.VMEM(a.shape, a.dtype) for a in out_shape] + [dma((2, count))],
            name="hand_on",
        )(*results)
        bound, down, up, out, qkv, gains, shifts, qv, out_vector, up_vector, down_vector, token = results
        boundary = bound.transpose(2, 0, 1, 3)
        parts = (boundary, token, gains, shifts, qkv.T[None], qv, out.T[None], out_vector, up.T[None])
        return (*parts, up_vector, down.reshape(block, 4 * width).T[None], down_vector)
    bound, grads, small = results
    me = lax.axis_index("dp")
    share = width // n
    token = lax.psum(small[12], ("dp", "section"))
    vectors = lax.psum(small[:12], "dp")
    wide = grads.astype(F32) * scale

    def scattered(first, count):
        part = wide[first * width : (first + count) * width]
        return lax.psum_scatter(part, "dp", scatter_dimension=0, tiled=True).T

    down = lax.psum_scatter(
        wide[: 4 * width].reshape(4, width, width), "dp", scatter_dimension=1, tiled=True
    )
    down = down.transpose(0, 2, 1).reshape(4 * width, share)
    up = scattered(UP, 4)
    out = scattered(OUT, 1)
    qkv = scattered(QKV, 3)

    def cut(first, count):
        return lax.dynamic_slice(vectors, (first, me * share), (count, share))

    up_vector = lax.dynamic_slice(vectors[7:11].reshape(-1), (me * 4 * share,), (4 * share,))
    parts = (bound.transpose(2, 0, 1, 3), token, cut(0, 2)[None], cut(2, 2)[None], qkv[None])
    parts += (cut(4, 2)[None], out[None], cut(6, 1), up[None], up_vector[None], down[None], cut(11, 1))
    return parts


def solution(mesh):
    return jax.shard_map(
        functools.partial(on_device, mesh.shape["dp"]),
        mesh=mesh,
        in_specs=(
            P("dp", None, None),
            P("dp", None),
            P(),
            P("section", None, None),
            P("section", None, None),
            P("section", None, None),
            P("section", None, None),
            P("section", None, None),
            P("section", None),
            P("section", None, None),
            P("section", None),
            P("section", None, None),
            P("section", None),
            P("dp", None, None),
        ),
        out_specs=(
            P("section", "dp", None, None),
            P(),
            P("section", None, "dp"),
            P("section", None, "dp"),
            P("section", None, "dp"),
            P("section", None, "dp"),
            P("section", None, "dp"),
            P("section", "dp"),
            P("section", None, "dp"),
            P("section", "dp"),
            P("section", None, "dp"),
            P("section", "dp"),
        ),
        check_vma=False,
    )
```

```python
import functools
import math

import jax
import jax.numpy as jnp
from jax import lax
from jax.experimental import pallas as pl
from jax.experimental.pallas import tpu as pltpu
from jax.sharding import PartitionSpec as P

HEADS = 12
EPS = 1e-06
BF = jnp.bfloat16
F32 = jnp.float32
Z_FIRST = 2
WINDOW = 4
LAG = (0, 1, 2, 3)
UNITS = 12
UP, OUT, QKV, DOWN_W = 4, 8, 9, 12
SMALL = 16
SMALL_AT = (1, 7, 9, 10, 11)
INV_SQRT2 = 1.0 / math.sqrt(2.0)
INV_SQRT2PI = 1.0 / math.sqrt(2.0 * math.pi)


def dot(a, b, contract_a, contract_b):
    return lax.dot_general(
        a, b, (((contract_a,), (contract_b,)), ((), ())), preferred_element_type=F32
    )


def fold8(x):
    rows, width = x.shape
    return jnp.sum(x.reshape(rows // 8, 8, width), axis=0)


def kernel(geo, *refs):
    (n, images, seq, pad, width, scale) = geo
    reduce_here = n == 16
    total_rows = images * pad
    block = width // 16
    names = ["patches", "cotangent", "mask", "token", "gains", "shifts", "qv_bias", "out_bias", "up_bias"]
    names += ["down_bias", "w_qkv", "w_out", "w_up", "w_down", "bound"]
    names += ["grads", "small"]
    names += ["wg", "x", "n1", "a1", "qkv", "o", "n2", "a2", "act", "gp", "dy", "send", "prob", "cols"]
    names += ["yb", "da", "tb", "do", "pin", "plain", "sm", "sms", "smr"]
    names += ["pin_sem", "w_sem", "out_sem", "fs", "fr", "bs", "br"]
    if reduce_here:
        names += ["stage", "rc", "ry", "zb", "zf", "cs", "cr", "ys", "yr", "rs", "rr", "ls", "lr", "ss", "sr", "put_sem"]
    r = dict(zip(names, refs, strict=True))
    wg = r["wg"]
    me = lax.axis_index("dp")
    sec = lax.axis_index("section")
    first, second = sec == 0, sec == 1

    def dp_at(bit):
        mine = lax.rem(me // bit, 2)
        return {"dp": me + bit - 2 * bit * mine, "section": sec}

    across = {"dp": me, "section": 1 - sec}
    core, y_at, z_at = lax.rem(me, 2), lax.rem(me // 2, 2), me // 4
    partners = [across]
    if reduce_here:
        partners += [dp_at(1), dp_at(2)]
        partners += [{"dp": lax.rem(me + 4 * turn, n), "section": sec} for turn in (1, 2, 3)]

    def unit_rows(unit, offset=0, size=width):
        return pl.ds(pl.multiple_of(unit * width + offset, 16), size)

    weight_copies = []
    for j in range(3):
        weight_copies.append((QKV + j, r["w_qkv"].at[0, :, pl.ds(width * j, width)]))
    weight_copies.append((OUT, r["w_out"].at[0]))
    for j in range(4):
        weight_copies.append((UP + j, r["w_up"].at[0, :, pl.ds(width * j, width)]))
    for j in range(4):
        weight_copies.append((DOWN_W + j, r["w_down"].at[0, pl.ds(width * j, width), :]))

    def weight_copy(index):
        unit, source = weight_copies[index]
        return pltpu.make_async_copy(source, wg.at[unit_rows(unit), :], r["w_sem"].at[index])

    def own_copy(source, img):
        return pltpu.make_async_copy(r[source].at[img], r["pin"].at[img], r["pin_sem"].at[img])

    @pl.when(first)
    def _():
        own_copy("patches", 0).start()

    @pl.when(second)
    def _():
        own_copy("cotangent", 0).start()

    for index in range(3):
        weight_copy(index).start()

    @pl.when(first)
    def _():
        for img in range(1, images):
            own_copy("patches", img).start()

    @pl.when(second)
    def _():
        for img in range(1, images):
            own_copy("cotangent", img).start()

    barrier = pltpu.get_barrier_semaphore()
    for partner in partners:
        pl.semaphore_signal(barrier, inc=1, device_id=partner)

    r["sm"][...] = jnp.zeros_like(r["sm"])

    def image_rows(img, offset=0, size=pad):
        return pl.ds(pl.multiple_of(img * pad + offset, 16), size)

    def forward_send(img):
        rows = image_rows(img)
        return pltpu.make_async_remote_copy(
            src_ref=r["send"].at[rows, :],
            dst_ref=r["x"].at[rows, :],
            send_sem=r["fs"].at[img],
            recv_sem=r["fr"].at[img],
            device_id=across,
        )

    def backward_send(img):
        rows = image_rows(img)
        return pltpu.make_async_remote_copy(
            src_ref=r["send"].at[rows, :],
            dst_ref=r["dy"].at[rows, :],
            send_sem=r["bs"].at[img],
            recv_sem=r["br"].at[img],
            device_id=across,
        )

    def bound_copy(img):
        return pltpu.make_async_copy(r["plain"].at[img], r["bound"].at[img], r["out_sem"].at[img])

    def write_bound(img, at, values):
        size = min(16, seq - at)
        r["plain"][img, at : at + size, 0, :] = values[:size]

    def row_blocks(img):
        return [image_rows(img, 16 * b, 16) for b in range(pad // 16)]

    def norm_forward(img, read, which, normed, scaled):
        gain = r["gains"][which : which + 1, :]
        shift = r["shifts"][which : which + 1, :]
        for b, rows in enumerate(row_blocks(img)):
            values = read(b, rows)
            centered = values - jnp.mean(values, axis=1, keepdims=True)
            variance = jnp.mean(centered * centered, axis=1, keepdims=True)
            inverse = lax.rsqrt(variance + EPS)
            unit = centered * inverse
            r["cols"][rows, which : which + 1] = inverse
            normed[rows, :] = unit.astype(BF)
            scaled[rows, :] = (unit * gain + shift).astype(BF)

    def halves(values):
        lane = lax.broadcasted_iota(jnp.int32, values.shape, 1)
        zero = jnp.zeros_like(values)
        low = lane < width // HEADS
        return jnp.where(low, values, zero), jnp.where(low, zero, values)

    def attention_forward(img, pair):
        rows = image_rows(img)
        lanes = pl.ds(128 * pair, 128)
        queries = r["qkv"][0, rows, lanes]
        keys = r["qkv"][1, rows, lanes]
        values = r["qkv"][2, rows, lanes]
        mixed = []
        for head, part in enumerate(halves(queries)):
            scores = dot(keys, part, 1, 1)
            key_at = lax.broadcasted_iota(jnp.int32, scores.shape, 0)
            scores = jnp.where(key_at < seq, scores, -1e30)
            raised = jnp.exp(scores - jnp.max(scores, axis=0, keepdims=True))
            share = 1.0 / jnp.sum(raised, axis=0, keepdims=True)
            prob = (raised * share).astype(BF)
            r["prob"][img * HEADS + 2 * pair + head] = prob
            mixed.append(dot(prob, values, 0, 0))
        lane = lax.broadcasted_iota(jnp.int32, mixed[0].shape, 1)
        r["o"][rows, lanes] = jnp.where(lane < width // HEADS, mixed[0], mixed[1]).astype(BF)

    def wait_weights(step, indices, then_start=()):
        @pl.when(step == 0)
        def _():
            for index in indices:
                weight_copy(index).wait()
            for index in then_start:
                weight_copy(index).start()

    def forward_stages(img, step=None):
        rows = image_rows(img)
        norm_forward(img, lambda b, at: r["x"][at, :].astype(F32), 0, r["n1"], r["a1"])
        yield
        if step is not None:
            wait_weights(step, range(0, 3), range(3, UNITS))
        for j in range(3):
            projected = dot(r["a1"][rows, :], wg[unit_rows(QKV + j), :], 1, 0)
            if j == 0:
                projected = (projected + r["qv_bias"][0:1, :]) * (1.0 / math.sqrt(width // HEADS))
            if j == 2:
                projected = projected + r["qv_bias"][1:2, :]
            r["qkv"][j, rows, :] = projected.astype(BF)
            yield
        for pair in range(HEADS // 2):
            attention_forward(img, pair)
            yield
        if step is not None:
            wait_weights(step, range(3, 4))
        r["yb"][...] = (
            r["x"][rows, :].astype(F32)
            + dot(r["o"][rows, :], wg[unit_rows(OUT), :], 1, 0)
            + r["out_bias"][...]
        )
        yield
        norm_forward(img, lambda b, at: r["yb"][16 * b : 16 * (b + 1), :], 1, r["n2"], r["a2"])
        yield
        if step is not None:
            wait_weights(step, range(4, UNITS))
        result = None
        for j in range(4):
            hidden = dot(r["a2"][rows, :], wg[unit_rows(UP + j), :], 1, 0)
            hidden = hidden + r["up_bias"][:, width * j : width * (j + 1)]
            below = 0.5 + 0.5 * lax.erf(hidden * INV_SQRT2)
            slope = below + hidden * (jnp.exp(hidden * hidden * -0.5) * INV_SQRT2PI)
            active = (hidden * below).astype(BF)
            r["act"][j, rows, :] = active
            r["gp"][j, rows, :] = slope.astype(BF)
            term = dot(active, wg[unit_rows(DOWN_W + j), :], 1, 0)
            result = term if result is None else result + term
            yield
        yield r["yb"][...] + result + r["down_bias"][...]

    def keep_result(img, result):
        for at in range(0, seq, 16):
            write_bound(img, at, result[at : at + 16])

    def forward(step, img):
        @pl.when(first)
        def _():
            tail = image_rows(img, seq // 16 * 16, 16)
            r["x"][tail, :] = jnp.zeros((16, width), BF)
            own_copy("patches", img).wait()
            row = r["mask"][pl.ds(img, 1), :]
            at_row = lax.broadcasted_iota(jnp.int32, (pad, seq), 0)
            at_lane = lax.broadcasted_iota(jnp.int32, (pad, seq), 1)
            covered = jnp.where((at_row == at_lane) & (row == 1), 1.0, 0.0)
            column = jnp.sum(covered, axis=1, keepdims=True)
            r["cols"][image_rows(img), 2:3] = column
            token = r["token"][...][None, :].astype(F32)
            kept = r["pin"][img].astype(F32)
            mixed = jnp.where(column[:seq] > 0.5, token, kept)
            r["x"][image_rows(img, 0, seq), :] = mixed.astype(BF)

        @pl.when(second & (step == 0))
        def _():
            for at in range(images):
                own_copy("cotangent", at).wait()
                tail = at * pad + seq // 16 * 16
                r["dy"][tail : tail + 16, :] = jnp.zeros((16, width), BF)
                r["dy"][at * pad : at * pad + seq, :] = r["pin"][at]

        @pl.when(second)
        def _():
            forward_send(img).wait_recv()

        for result in forward_stages(img, step):
            pass

        @pl.when(step == 0)
        def _():
            pl.semaphore_wait(barrier, len(partners))

        @pl.when(first)
        def _():
            r["send"][image_rows(img), :] = result.astype(BF)
            forward_send(img).start()

        @pl.when(second)
        def _():
            keep_result(img, result)

    def norm_backward(img, which, gradient, incoming):
        results = []
        gain = r["gains"][which : which + 1, :]
        normed = r["n1"] if which == 0 else r["n2"]
        gain_sum = jnp.zeros((8, width), F32)
        shift_sum = jnp.zeros((8, width), F32)
        for b, rows in enumerate(row_blocks(img)):
            here = gradient[16 * b : 16 * (b + 1), :]
            unit = normed[rows, :].astype(F32)
            gain_sum = gain_sum + fold8(here * unit)
            shift_sum = shift_sum + fold8(here)
            scaled = here * gain
            mean = jnp.mean(scaled, axis=1, keepdims=True)
            along = jnp.mean(scaled * unit, axis=1, keepdims=True)
            local = (scaled - mean - unit * along) * r["cols"][rows, which : which + 1]
            results.append((b, rows, local + incoming(b, rows)))
        r["sm"][which : which + 1, :] += jnp.sum(gain_sum, axis=0, keepdims=True)
        r["sm"][2 + which : 3 + which, :] += jnp.sum(shift_sum, axis=0, keepdims=True)
        return results

    def backward_mlp_stages(img):
        rows = image_rows(img)
        incoming = r["dy"][rows, :]
        r["sm"][11:12, :] += jnp.sum(incoming.astype(F32), axis=0, keepdims=True)
        back = None
        for j in range(4):
            change = dot(incoming, wg[unit_rows(DOWN_W + j), :], 1, 1)
            change = change * r["gp"][j, rows, :].astype(F32)
            r["sm"][7 + j : 8 + j, :] += jnp.sum(change, axis=0, keepdims=True)
            narrow = change.astype(BF)
            r["gp"][j, rows, :] = narrow
            term = dot(narrow, wg[unit_rows(UP + j), :], 1, 1)
            back = term if back is None else back + term
            yield
        r["tb"][...] = back
        bias_sum = jnp.zeros((8, width), F32)
        for b, block_rows, middle in norm_backward(
            img, 1, r["tb"], lambda b, block_rows: r["dy"][block_rows, :].astype(F32)
        ):
            bias_sum = bias_sum + fold8(middle)
            r["da"][16 * b : 16 * (b + 1), :] = middle
            r["n2"][block_rows, :] = middle.astype(BF)
        r["sm"][6:7, :] += jnp.sum(bias_sum, axis=0, keepdims=True)
        yield

    def attention_backward_stages(img, pairs):
        rows = image_rows(img)
        places = [pl.ds(128 * pair, 128) for pair in pairs]
        loaded = []
        for pair, lanes in zip(pairs, places):
            probs = [r["prob"][img * HEADS + 2 * pair + head] for head in range(2)]
            loaded.append((*[r["qkv"][i, rows, lanes] for i in range(3)], r["do"][:, lanes], probs))
        results = []
        for queries, keys, values, back, probs in loaded:
            query_parts, key_parts, back_parts = halves(queries), halves(keys), halves(back)
            total = None
            for head in range(2):
                wide = probs[head].astype(F32)
                change = dot(values, back_parts[head], 1, 1)
                carried = jnp.sum(wide * change, axis=0, keepdims=True)
                scores = (wide * (change - carried)).astype(BF)
                terms = (
                    dot(scores, key_parts[head], 0, 0),
                    dot(scores, query_parts[head], 1, 0),
                    dot(probs[head], back_parts[head], 1, 0),
                )
                total = terms if total is None else [a + b for a, b in zip(total, terms)]
            d_query, d_key, d_value = total
            results.append((d_query * (1.0 / math.sqrt(width // HEADS)), d_key, d_value))
            yield
        for (d_query, d_key, d_value), lanes in zip(results, places):
            r["sm"][4:5, lanes] += jnp.sum(d_query, axis=0, keepdims=True)
            r["sm"][5:6, lanes] += jnp.sum(d_value, axis=0, keepdims=True)
            r["qkv"][0, rows, lanes] = d_query.astype(BF)
            r["qkv"][1, rows, lanes] = d_key.astype(BF)
            r["qkv"][2, rows, lanes] = d_value.astype(BF)

    def backward_attention_stages(img):
        rows = image_rows(img)
        r["do"][...] = dot(r["n2"][rows, :], wg[unit_rows(OUT), :], 1, 1).astype(BF)
        yield
        yield from attention_backward_stages(img, range(HEADS // 2))
        yield
        back = None
        for j in range(3):
            term = dot(r["qkv"][j, rows, :], wg[unit_rows(QKV + j), :], 1, 1)
            back = term if back is None else back + term
            yield
        r["tb"][...] = back
        for b, block_rows, entry in norm_backward(
            img, 0, r["tb"], lambda b, block_rows: r["da"][16 * b : 16 * (b + 1), :]
        ):
            r["da"][16 * b : 16 * (b + 1), :] = entry
        yield

    def send_back(img):
        r["send"][image_rows(img), :] = r["da"][...].astype(BF)
        backward_send(img).start()

    def run(stages):
        for _ in stages:
            pass

    def backward_attention(img):
        run(backward_attention_stages(img))

        @pl.when(first)
        def _():
            token_sum = jnp.zeros((8, width), F32)
            for b, block_rows in enumerate(row_blocks(img)):
                entry = r["da"][16 * b : 16 * (b + 1), :]
                under = r["cols"][block_rows, 2:3] > 0.5
                token_sum = token_sum + fold8(jnp.where(under, entry, 0.0))
                if 16 * b < seq:
                    write_bound(img, 16 * b, jnp.where(under, 0.0, entry))
            r["sm"][12:13, :] += jnp.sum(token_sum, axis=0, keepdims=True)

        @pl.when(second)
        def _():
            send_back(img)

    half_rows, quarter = width // 2, width // 4
    across_core, across_y = dp_at(1), dp_at(2)

    def core_copy(unit):
        return pltpu.make_async_remote_copy(
            src_ref=wg.at[unit_rows(unit, half_rows * (1 - core), half_rows), :],
            dst_ref=r["rc"].at[pl.ds(pl.multiple_of(unit * half_rows, 16), half_rows), :],
            send_sem=r["cs"].at[unit],
            recv_sem=r["cr"].at[unit],
            device_id=across_core,
        )

    in_order = UNITS - Z_FIRST

    def y_slot(unit, z_first):
        if z_first:
            at = in_order * quarter + unit // 4 * block
            return r["ry"].at[pl.ds(pl.multiple_of(at, 16), block), :]
        return r["ry"].at[pl.ds(pl.multiple_of(index_of(unit) * quarter, 16), quarter), :]

    def index_of(unit):
        return unit - 1 - jnp.minimum(unit // 4, Z_FIRST - 1)

    def unit_at(index):
        return index + 1 + jnp.minimum(index // 3, Z_FIRST - 1)

    def y_copy(unit, z_first, part=0):
        landing = y_slot(unit, z_first)
        if z_first:
            size, away = block, half_rows * core + 2 * block * z_at + block * (1 - y_at)
        else:
            size = 2 * block
            away = half_rows * core + quarter * (1 - y_at) + size * part
            landing = landing.at[pl.ds(size * part, size), :]
        return pltpu.make_async_remote_copy(
            src_ref=wg.at[unit_rows(unit, away, size), :],
            dst_ref=landing,
            send_sem=r["ys"].at[2 * unit + part],
            recv_sem=r["yr"].at[2 * unit + part],
            device_id=across_y,
        )

    def z_rows(unit, owner, z_first):
        if z_first:
            return unit_rows(unit, half_rows * core + 2 * block * owner, 2 * block)
        at = (0, 2, 3, 1)[owner]
        return unit_rows(unit, half_rows * core + quarter * y_at + block * at, block)

    def z_slot(unit, slot, z_first):
        if z_first:
            at = unit // 4 * 10 * block + slot * 2 * block
            return r["zf"].at[pl.ds(pl.multiple_of(at, 16), 2 * block), :]
        at = index_of(unit) * 5 * block + slot * block
        return r["zb"].at[pl.ds(pl.multiple_of(at, 16), block), :]

    def z_copy(unit, owner, toward, z_first, goes_to):
        up = toward > 0
        slot = owner if up or owner != goes_to else 4
        return pltpu.make_async_remote_copy(
            src_ref=wg.at[z_rows(unit, owner, z_first), :],
            dst_ref=z_slot(unit, slot, z_first),
            send_sem=r["rs" if up else "ls"].at[unit * 4 + owner],
            recv_sem=r["rr" if up else "lr"].at[unit * 4 + owner],
            device_id={"dp": lax.rem(me + n + 4 * toward, n), "section": sec},
        )

    def add_rows(unit, offset, source, size):
        for part in range(size // block):
            rows = unit_rows(unit, offset + block * part, block)
            came = source[block * part : block * (part + 1), :]
            wg[rows, :] = (wg[rows, :].astype(F32) + came.astype(F32)).astype(BF)

    def add_core(unit, z_first):
        core_copy(unit).wait_recv()
        came = r["rc"].at[pl.ds(pl.multiple_of(unit * half_rows, 16), half_rows), :]
        add_rows(unit, half_rows * core, came, half_rows)
        if z_first:
            z_start(unit, True)
        else:
            for part in range(2):
                y_copy(unit, False, part).start()

    def z_start(unit, z_first, from_bottom=(3, 2, 1), from_top=(0, 1, 2)):
        @pl.when(z_at == 0)
        def _():
            for owner in from_bottom:
                z_copy(unit, owner, 1, z_first, 1).start()

        @pl.when(z_at == 3)
        def _():
            for owner in from_top:
                z_copy(unit, owner, -1, z_first, 2).start()

    def z_hop(hop, unit, z_first):
        size = 2 * block if z_first else block

        def pass_on(here, owner, toward):
            z_copy(unit, owner, toward, z_first, here).wait_recv()
            rows = z_rows(unit, owner, z_first)
            came = z_slot(unit, owner, z_first)
            wg[rows, :] = (wg[rows, :].astype(F32) + came[...].astype(F32)).astype(BF)
            z_copy(unit, owner, toward, z_first, here + toward).start()

        def finish(here):
            total = wg[z_rows(unit, here, z_first), :].astype(F32)
            if here > 0:
                z_copy(unit, here, 1, z_first, here).wait_recv()
                total = total + z_slot(unit, here, z_first)[...].astype(F32)
            if here < 3:
                z_copy(unit, here, -1, z_first, here).wait_recv()
                total = total + z_slot(unit, 4, z_first)[...].astype(F32)
            if z_first:
                wg[z_rows(unit, here, True), :] = total.astype(BF)
            else:
                put(unit, total)

        @pl.when(z_at == hop)
        def _():
            for owner in range(3, hop, -1):
                pass_on(hop, owner, 1)
            if hop >= 2:
                finish(hop)

        @pl.when(z_at == 3 - hop)
        def _():
            for owner in range(3 - hop):
                pass_on(3 - hop, owner, -1)
            if hop >= 2:
                finish(3 - hop)

    def put_copy(unit):
        return pltpu.make_async_copy(r["stage"].at[unit], r["grads"].at[unit], r["put_sem"].at[unit])

    def put(unit, total):
        r["stage"][unit] = total * scale
        put_copy(unit).start()

    def finish_z_first(unit):
        y_copy(unit, True).wait_recv()
        mine = unit_rows(unit, half_rows * core + 2 * block * z_at + block * y_at, block)
        came = y_slot(unit, True)[...]
        put(unit, wg[mine, :].astype(F32) + came.astype(F32))

    def add_y(unit):
        size = 2 * block
        for part in range(2):
            y_copy(unit, False, part).wait_recv()
            came = y_slot(unit, False).at[pl.ds(size * part, size), :]
            add_rows(unit, half_rows * core + quarter * y_at + size * part, came, size)
            if part == 0:
                z_start(unit, False, (3,), (0,))
            else:
                z_start(unit, False, (2, 1), (1, 2))

    def place(owner, z_first):
        core_of, y_of, z_of = lax.rem(owner, 2), lax.rem(owner // 2, 2), owner // 4
        if z_first:
            return core_of * 8 + z_of * 2 + y_of
        return core_of * 8 + y_of * 4 + jnp.where(z_of == 0, 0, jnp.where(z_of == 3, 1, z_of + 1))

    def weight_gradient(left, right, chunk, first_unit, spread, z_first=False):
        for half in range(2):
            product = dot(left(half), right, 0, 0).astype(BF)
            for b in range(8):
                at = chunk * 16 + 8 * half + b
                if spread == 1:
                    at = 8 * half + b
                if reduce_here:
                    owner, part = at // spread, lax.rem(at, spread)
                    if spread == 4:
                        part = b % spread
                        z_first = part == 0
                    rows = unit_rows(first_unit + part, place(owner, z_first) * block, block)
                else:
                    rows = unit_rows(first_unit, at * block, block)
                wg[rows, :] = product[block * b : block * (b + 1), :]

    def half_lanes(half):
        return pl.ds((width // 2) * half, width // 2)

    def down_gradient():
        def one(z_first):
            def body(j, carry):
                weight_gradient(
                    lambda half: r["dy"][:, half_lanes(half)], r["act"][j], j, j, 1, z_first
                )
                if reduce_here:
                    core_copy(j).start()
                    if not z_first:
                        pl.when(j == 1)(lambda: add_core(0, True))
                        pl.when(j > 1)(lambda: add_core(j - 1, False))
                return carry

            return body

        lax.fori_loop(0, 1, one(True), 0)
        lax.fori_loop(1, 4, one(False), 0)
        if reduce_here:
            add_core(3, False)

    def start_units(begin, end):
        if reduce_here:
            for unit in range(begin, end):
                core_copy(unit).start()

    def add_y_if(when, unit):
        if reduce_here:
            pl.when(when)(lambda: add_y(unit))

    def turn(step, carry):
        img = lax.rem(step, images)
        early = step < images
        back_now = early == second
        down_now = step == jnp.where(first, 2 * images - 1, images)

        @pl.when(early)
        def _():
            forward(step, img)

        @pl.when(back_now & first)
        def _():
            backward_send(img).wait_recv()

        @pl.when(down_now)
        def _():
            down_gradient()

        @pl.when(back_now)
        def _():
            run(backward_mlp_stages(img))

        @pl.when(back_now)
        def _():
            backward_attention(img)

        return carry

    lax.fori_loop(0, 2 * images, turn, 0)

    def up_one(c, carry):
        weight_gradient(lambda half: r["gp"][c, :, half_lanes(half)], r["a2"][...], c, UP, 4)
        return carry

    add_y_if(first, 1)
    lax.fori_loop(0, 4, up_one, 0)
    start_units(UP, OUT)
    if reduce_here:
        add_core(UP, True)
        for unit in range(UP + 1, OUT):
            add_core(unit, False)
    add_y_if(first, 2)
    add_y_if(second, 1)
    weight_gradient(lambda half: r["n2"][:, half_lanes(half)], r["o"][...], 0, OUT, 1, Z_FIRST == 3)
    start_units(OUT, QKV)

    def qkv_one(c, carry):
        weight_gradient(lambda half: r["qkv"][c, :, half_lanes(half)], r["a1"][...], c, QKV, 3)
        return carry

    lax.fori_loop(0, 3, qkv_one, 0)
    start_units(QKV, UNITS)
    if reduce_here and Z_FIRST == 3:
        add_core(OUT, True)

    for img in range(images):
        bound_copy(img).start()

    def finish_images():
        for img in range(images):
            bound_copy(img).wait()

            @pl.when(first)
            def _(img=img):
                forward_send(img).wait_send()

            @pl.when(second)
            def _(img=img):
                backward_send(img).wait_send()

    if reduce_here:
        hops = [dp_at(1), dp_at(2), dp_at(8), dp_at(4), across]

        def small_send(t):
            return pltpu.make_async_remote_copy(
                src_ref=r["sms"].at[t],
                dst_ref=r["smr"].at[t],
                send_sem=r["ss"].at[t],
                recv_sem=r["sr"].at[t],
                device_id=hops[t],
            )

        r["sms"][0] = r["sm"][...]
        small_send(0).start()

        def small_step(t):
            small_send(t).wait_recv()
            if t < 4:
                r["sms"][t + 1] = r["sms"][t] + r["smr"][t]
                small_send(t + 1).start()
                return
            total = r["sms"][4] * scale
            shift = lax.rem(width - block * me, width)
            r["small"][...] = pltpu.roll(total, shift, 1)
            r["small"][12:13, :] = (r["sms"][4, 12:13, :] + r["smr"][4, 12:13, :]) * scale
            up_row = r["sms"][4, pl.ds(7 + me // 4, 1), :] * scale
            up_shift = lax.rem(width - 4 * block * lax.rem(me, 4), width)
            spread_row = jnp.broadcast_to(up_row, (8, width))
            r["small"][13:14, :] = pltpu.roll(spread_row, up_shift, 1)[0:1]

        def sent(unit, z_first):
            core_copy(unit).wait_send()
            for part in range(1 if z_first else 2):
                y_copy(unit, z_first, part).wait_send()
            for here in range(4):

                @pl.when(z_at == here)
                def _(here=here):
                    for owner in range(4):
                        if owner > here:
                            z_copy(unit, owner, 1, z_first, here + 1).wait_send()
                        if owner < here:
                            z_copy(unit, owner, -1, z_first, here - 1).wait_send()

            put_copy(unit).wait()

        def drain(k, carry):
            @pl.when((k < in_order) & ((k > 1) | second))
            def _():
                add_y(unit_at(k))

            @pl.when((k > 1) & (k + WINDOW < in_order))
            def _():
                add_core(unit_at(k + WINDOW), False)

            for hop in (1, 2, 3):

                @pl.when((k >= LAG[hop]) & (k < LAG[hop] + Z_FIRST))
                def _(hop=hop):
                    z_hop(hop, 4 * (k - LAG[hop]), True)

            for hop in (1, 2, 3):

                @pl.when((k >= LAG[hop]) & (k < in_order + LAG[hop]))
                def _(hop=hop):
                    z_hop(hop, unit_at(k - LAG[hop]), False)

            for t in range(5):

                @pl.when(k == SMALL_AT[t])
                def _(t=t):
                    small_step(t)

            @pl.when((k >= LAG[3] + 1) & (k < LAG[3] + 1 + Z_FIRST))
            def _():
                y_copy(4 * (k - LAG[3] - 1), True).start()

            @pl.when((k >= in_order) & (k < in_order + Z_FIRST))
            def _():
                finish_z_first(4 * (k - in_order))

            @pl.when(k == 3)
            def _():
                finish_images()

            @pl.when(k >= LAG[3] + 2)
            def _():
                sent(unit_at(k - LAG[3] - 2), False)

            return carry

        lax.fori_loop(1, in_order + LAG[3], drain, 0)

        for unit in range(0, 4 * Z_FIRST, 4):
            sent(unit, True)
        for index in range(in_order - 2, in_order):
            sent(unit_at(index), False)
        for t in range(5):
            small_send(t).wait_send()
    else:
        r["small"][...] = r["sm"][...] * scale
        out = pltpu.make_async_copy(wg.at[pl.ds(0, UNITS * width), :], r["grads"], r["pin_sem"].at[0])
        out.start()
        out.wait()
        finish_images()


def hand_on(bound, grads, small, *refs):
    out_bound, down, up, out, three = refs[:5]
    vectors = refs[5:12]
    held_bound, held_grads, held_small = refs[12:15]
    held_vectors = refs[15:22]
    load_sem, store_sem, small_sem, vector_sem = refs[22:]
    images = bound.shape[0]
    units, block, width = grads.shape

    def target(unit):
        if unit < UP:
            return down.at[:, pl.ds(width * unit, width)]
        if unit < OUT:
            return up.at[pl.ds(block * (unit - UP), block), :]
        if unit < QKV:
            return out
        return three.at[pl.ds(block * (unit - QKV), block), :]

    moves = [(bound.at[i], held_bound.at[i], out_bound.at[i]) for i in range(images)]
    moves += [(grads.at[unit], held_grads.at[unit], target(unit)) for unit in range(units)]
    loads = [
        pltpu.make_async_copy(source, held, load_sem.at[i])
        for i, (source, held, _) in enumerate(moves)
    ]
    stores = [
        pltpu.make_async_copy(held, result, store_sem.at[i])
        for i, (_, held, result) in enumerate(moves)
    ]
    load_small = pltpu.make_async_copy(small, held_small, small_sem)
    vector_stores = [
        pltpu.make_async_copy(held, result, vector_sem.at[i])
        for i, (held, result) in enumerate(zip(held_vectors, vectors))
    ]
    load_small.start()
    for load in loads:
        load.start()
    load_small.wait()
    gains, shifts, qv, out_vector, up_vector, down_vector, token = held_vectors
    gains[0] = held_small[0:2, :block]
    shifts[0] = held_small[2:4, :block]
    qv[0] = held_small[4:6, :block]
    out_vector[...] = held_small[6:7, :block]
    down_vector[...] = held_small[11:12, :block]
    up_vector[...] = held_small[13:14, : 4 * block]
    token[...] = held_small[12:13, :].reshape(width)
    for store in vector_stores:
        store.start()
    for load, store in zip(loads, stores):
        load.wait()
        store.start()
    for store in stores + vector_stores:
        store.wait()


def on_device(n, *args):
    (patches, block_mask, mask_token, norm_gains, norm_shifts, w_qkv, qv_bias, w_out, out_bias) = args[:9]
    w_up, up_bias, w_down, down_bias, cotangent = args[9:]
    images, seq, width = patches.shape
    pad = -(-seq // 16) * 16
    rows = images * pad
    reduce_here = n == 16
    scale = 1.0 / math.sqrt(images * n * seq)
    geo = (n, images, seq, pad, width, scale)
    block = width // 16
    anywhere = pl.BlockSpec(memory_space=pl.ANY)
    vmem = pl.BlockSpec(memory_space=pltpu.VMEM)
    bound_shape = jax.ShapeDtypeStruct((images, seq, 1, width), F32)
    if reduce_here:
        grads_shape = jax.ShapeDtypeStruct((UNITS, block, width), F32)
    else:
        grads_shape = jax.ShapeDtypeStruct((UNITS * width, width), BF)
    out_shape = [bound_shape, grads_shape, jax.ShapeDtypeStruct((SMALL, width), F32)]
    narrow = pltpu.VMEM((rows, width), BF)
    dma = pltpu.SemaphoreType.DMA
    scratch = [
        pltpu.VMEM((16 * width, width), BF),
        narrow,
        narrow,
        narrow,
        pltpu.VMEM((3, rows, width), BF),
        narrow,
        narrow,
        narrow,
        pltpu.VMEM((4, rows, width), BF),
        pltpu.VMEM((4, rows, width), BF),
        narrow,
        narrow,
        pltpu.VMEM((images * HEADS, pad, pad), BF),
        pltpu.VMEM((rows, 3), F32),
        pltpu.VMEM((pad, width), F32),
        pltpu.VMEM((pad, width), F32),
        pltpu.VMEM((pad, width), F32),
        pltpu.VMEM((pad, width), BF),
        pltpu.VMEM((images, seq, width), BF),
        pltpu.VMEM((images, seq, 1, width), F32),
        pltpu.VMEM((SMALL, width), F32),
        pltpu.VMEM((5, SMALL, width), F32),
        pltpu.VMEM((5, SMALL, width), F32),
        dma((images,)),
        dma((UNITS,)),
        dma((images,)),
        dma((images,)),
        dma((images,)),
        dma((images,)),
        dma((images,)),
    ]
    if reduce_here:
        scratch += [
            pltpu.VMEM((UNITS, block, width), F32),
            pltpu.VMEM((UNITS * width // 2, width), BF),
            pltpu.VMEM((((UNITS - Z_FIRST) * 4 + Z_FIRST) * block, width), BF),
            pltpu.VMEM(((UNITS - Z_FIRST) * 5 * block, width), BF),
            pltpu.VMEM((Z_FIRST * 10 * block, width), BF),
        ]
        scratch += [dma((UNITS,))] * 2 + [dma((UNITS * 2,))] * 2 + [dma((UNITS * 4,))] * 4 + [dma((5,))] * 2 + [dma((UNITS,))]
    weights = 12 * width * width
    bound, grads, small = pl.pallas_call(
        functools.partial(kernel, geo),
        out_shape=out_shape,
        in_specs=[anywhere] * 2 + [vmem] * 8 + [anywhere] * 4,
        out_specs=[anywhere, anywhere, vmem],
        scratch_shapes=scratch,
        compiler_params=pltpu.CompilerParams(
            collective_id=0, has_side_effects=True, vmem_limit_bytes=64 * 1024 * 1024 - 65536
        ),
        cost_estimate=pl.CostEstimate(
            flops=6 * rows * weights, bytes_accessed=4 * weights, transcendentals=rows * width * 8
        ),
        name="relay",
    )(
        patches,
        cotangent,
        block_mask,
        mask_token,
        norm_gains[0],
        norm_shifts[0],
        qv_bias[0],
        out_bias,
        up_bias,
        down_bias,
        w_qkv,
        w_out,
        w_up,
        w_down,
    )
    if reduce_here:
        shapes = [(block, 4 * width), (4 * block, width), (block, width), (3 * block, width)]
        shapes += [(1, 2, block)] * 3 + [(1, block), (1, 4 * block), (1, block), (width,)]
        results = pl.pallas_call(
            hand_on,
            out_shape=[bound_shape] + [jax.ShapeDtypeStruct(shape, F32) for shape in shapes],
            in_specs=[anywhere] * 3,
            out_specs=[anywhere] * 12,
            scratch_shapes=[
                pltpu.VMEM(bound_shape.shape, F32),
                pltpu.VMEM(grads_shape.shape, F32),
                pltpu.VMEM((SMALL, width), F32),
                *[pltpu.VMEM(shape, F32) for shape in shapes[4:]],
                dma((images + UNITS,)),
                dma((images + UNITS,)),
                dma(()),
                dma((len(shapes) - 4,)),
            ],
            name="hand_on",
        )(bound, grads, small)
        bound, down, up, out, qkv, gains, shifts, qv, out_vector, up_vector, down_vector, token = results
        boundary = bound.transpose(2, 0, 1, 3)
        parts = (boundary, token, gains, shifts, qkv.T[None], qv, out.T[None], out_vector, up.T[None])
        return (*parts, up_vector, down.T[None], down_vector)
    me = lax.axis_index("dp")
    share = width // n
    token = lax.psum(small[12], ("dp", "section"))
    vectors = lax.psum(small[:12], "dp")
    wide = grads.astype(F32) * scale

    def scattered(first, count):
        part = wide[first * width : (first + count) * width]
        return lax.psum_scatter(part, "dp", scatter_dimension=0, tiled=True).T

    down = lax.psum_scatter(
        wide[: 4 * width].reshape(4, width, width), "dp", scatter_dimension=1, tiled=True
    )
    down = down.transpose(0, 2, 1).reshape(4 * width, share)
    up = scattered(UP, 4)
    out = scattered(OUT, 1)
    qkv = scattered(QKV, 3)

    def cut(first, count):
        return lax.dynamic_slice(vectors, (first, me * share), (count, share))

    up_vector = lax.dynamic_slice(vectors[7:11].reshape(-1), (me * 4 * share,), (4 * share,))
    parts = (bound.transpose(2, 0, 1, 3), token, cut(0, 2)[None], cut(2, 2)[None], qkv[None])
    parts += (cut(4, 2)[None], out[None], cut(6, 1), up[None], up_vector[None], down[None], cut(11, 1))
    return parts


def solution(mesh):
    return jax.shard_map(
        functools.partial(on_device, mesh.shape["dp"]),
        mesh=mesh,
        in_specs=(
            P("dp", None, None),
            P("dp", None),
            P(),
            P("section", None, None),
            P("section", None, None),
            P("section", None, None),
            P("section", None, None),
            P("section", None, None),
            P("section", None),
            P("section", None, None),
            P("section", None),
            P("section", None, None),
            P("section", None),
            P("dp", None, None),
        ),
        out_specs=(
            P("section", "dp", None, None),
            P(),
            P("section", None, "dp"),
            P("section", None, "dp"),
            P("section", None, "dp"),
            P("section", None, "dp"),
            P("section", None, "dp"),
            P("section", "dp"),
            P("section", None, "dp"),
            P("section", "dp"),
            P("section", None, "dp"),
            P("section", "dp"),
        ),
        check_vma=False,
    )
```

```python
import functools
import math

import jax
import jax.numpy as jnp
from jax import lax
from jax.experimental import pallas as pl
from jax.experimental.pallas import tpu as pltpu
from jax.sharding import PartitionSpec as P

HEADS = 12
EPS = 1e-06
BF = jnp.bfloat16
F32 = jnp.float32
Z_FIRST = 2
WINDOW = 4
LAG = (0, 1, 3, 5)
UNITS = 12
UP, OUT, QKV, DOWN_W = 4, 8, 9, 12
SMALL = 16
SMALL_AT = (1, 7, 10, 12, 13)
INV_SQRT2 = 1.0 / math.sqrt(2.0)
INV_SQRT2PI = 1.0 / math.sqrt(2.0 * math.pi)


def dot(a, b, contract_a, contract_b):
    return lax.dot_general(
        a, b, (((contract_a,), (contract_b,)), ((), ())), preferred_element_type=F32
    )


def fold8(x):
    rows, width = x.shape
    return jnp.sum(x.reshape(rows // 8, 8, width), axis=0)


def kernel(geo, *refs):
    (n, images, seq, pad, width, scale) = geo
    reduce_here = n == 16
    total_rows = images * pad
    block = width // 16
    names = ["patches", "cotangent", "mask", "token", "gains", "shifts", "qv_bias", "out_bias", "up_bias"]
    names += ["down_bias", "w_qkv", "w_out", "w_up", "w_down", "bound"]
    names += ["grads", "small"]
    names += ["wg", "x", "n1", "a1", "qkv", "o", "n2", "a2", "act", "gp", "dy", "send", "prob", "cols"]
    names += ["yb", "da", "tb", "do", "pin", "plain", "sm", "sms", "smr"]
    names += ["pin_sem", "w_sem", "out_sem", "fs", "fr", "bs", "br"]
    if reduce_here:
        names += ["stage", "rc", "ry", "zb", "zf", "cs", "cr", "ys", "yr", "rs", "rr", "ls", "lr", "ss", "sr", "put_sem"]
    r = dict(zip(names, refs, strict=True))
    wg = r["wg"]
    me = lax.axis_index("dp")
    sec = lax.axis_index("section")
    first, second = sec == 0, sec == 1

    def dp_at(bit):
        mine = lax.rem(me // bit, 2)
        return {"dp": me + bit - 2 * bit * mine, "section": sec}

    across = {"dp": me, "section": 1 - sec}
    core, y_at, z_at = lax.rem(me, 2), lax.rem(me // 2, 2), me // 4
    partners = [across]
    if reduce_here:
        partners += [dp_at(1), dp_at(2)]
        partners += [{"dp": lax.rem(me + 4 * turn, n), "section": sec} for turn in (1, 2, 3)]

    def unit_rows(unit, offset=0, size=width):
        return pl.ds(pl.multiple_of(unit * width + offset, 16), size)

    weight_copies = []
    for j in range(3):
        weight_copies.append((QKV + j, r["w_qkv"].at[0, :, pl.ds(width * j, width)]))
    weight_copies.append((OUT, r["w_out"].at[0]))
    for j in range(4):
        weight_copies.append((UP + j, r["w_up"].at[0, :, pl.ds(width * j, width)]))
    for j in range(4):
        weight_copies.append((DOWN_W + j, r["w_down"].at[0, pl.ds(width * j, width), :]))

    def weight_copy(index):
        unit, source = weight_copies[index]
        return pltpu.make_async_copy(source, wg.at[unit_rows(unit), :], r["w_sem"].at[index])

    def own_copy(source, img):
        return pltpu.make_async_copy(r[source].at[img], r["pin"].at[img], r["pin_sem"].at[img])

    @pl.when(first)
    def _():
        own_copy("patches", 0).start()

    @pl.when(second)
    def _():
        own_copy("cotangent", 0).start()

    for index in range(3):
        weight_copy(index).start()

    @pl.when(first)
    def _():
        for img in range(1, images):
            own_copy("patches", img).start()

    @pl.when(second)
    def _():
        for img in range(1, images):
            own_copy("cotangent", img).start()

    barrier = pltpu.get_barrier_semaphore()
    for partner in partners:
        pl.semaphore_signal(barrier, inc=1, device_id=partner)

    r["sm"][...] = jnp.zeros_like(r["sm"])

    def image_rows(img, offset=0, size=pad):
        return pl.ds(pl.multiple_of(img * pad + offset, 16), size)

    def forward_send(img):
        rows = image_rows(img)
        return pltpu.make_async_remote_copy(
            src_ref=r["send"].at[rows, :],
            dst_ref=r["x"].at[rows, :],
            send_sem=r["fs"].at[img],
            recv_sem=r["fr"].at[img],
            device_id=across,
        )

    def backward_send(img):
        rows = image_rows(img)
        return pltpu.make_async_remote_copy(
            src_ref=r["send"].at[rows, :],
            dst_ref=r["dy"].at[rows, :],
            send_sem=r["bs"].at[img],
            recv_sem=r["br"].at[img],
            device_id=across,
        )

    def bound_copy(img):
        return pltpu.make_async_copy(r["plain"].at[img], r["bound"].at[img], r["out_sem"].at[img])

    def write_bound(img, at, values):
        size = min(16, seq - at)
        r["plain"][img, at : at + size, 0, :] = values[:size]

    def row_blocks(img):
        return [image_rows(img, 16 * b, 16) for b in range(pad // 16)]

    def norm_forward(img, read, which, normed, scaled):
        gain = r["gains"][which : which + 1, :]
        shift = r["shifts"][which : which + 1, :]
        for b, rows in enumerate(row_blocks(img)):
            values = read(b, rows)
            centered = values - jnp.mean(values, axis=1, keepdims=True)
            variance = jnp.mean(centered * centered, axis=1, keepdims=True)
            inverse = lax.rsqrt(variance + EPS)
            unit = centered * inverse
            r["cols"][rows, which : which + 1] = inverse
            normed[rows, :] = unit.astype(BF)
            scaled[rows, :] = (unit * gain + shift).astype(BF)

    def halves(values):
        lane = lax.broadcasted_iota(jnp.int32, values.shape, 1)
        zero = jnp.zeros_like(values)
        low = lane < width // HEADS
        return jnp.where(low, values, zero), jnp.where(low, zero, values)

    def attention_forward(img, pair):
        rows = image_rows(img)
        lanes = pl.ds(128 * pair, 128)
        queries = r["qkv"][0, rows, lanes]
        keys = r["qkv"][1, rows, lanes]
        values = r["qkv"][2, rows, lanes]
        mixed = []
        for head, part in enumerate(halves(queries)):
            scores = dot(keys, part, 1, 1)
            key_at = lax.broadcasted_iota(jnp.int32, scores.shape, 0)
            scores = jnp.where(key_at < seq, scores, -1e30)
            raised = jnp.exp(scores - jnp.max(scores, axis=0, keepdims=True))
            share = 1.0 / jnp.sum(raised, axis=0, keepdims=True)
            prob = (raised * share).astype(BF)
            r["prob"][img * HEADS + 2 * pair + head] = prob
            mixed.append(dot(prob, values, 0, 0))
        lane = lax.broadcasted_iota(jnp.int32, mixed[0].shape, 1)
        r["o"][rows, lanes] = jnp.where(lane < width // HEADS, mixed[0], mixed[1]).astype(BF)

    def wait_weights(step, indices, then_start=()):
        @pl.when(step == 0)
        def _():
            for index in indices:
                weight_copy(index).wait()
            for index in then_start:
                weight_copy(index).start()

    def forward_stages(img, step=None):
        rows = image_rows(img)
        norm_forward(img, lambda b, at: r["x"][at, :].astype(F32), 0, r["n1"], r["a1"])
        yield
        if step is not None:
            wait_weights(step, range(0, 3), range(3, UNITS))
        for j in range(3):
            projected = dot(r["a1"][rows, :], wg[unit_rows(QKV + j), :], 1, 0)
            if j == 0:
                projected = (projected + r["qv_bias"][0:1, :]) * (1.0 / math.sqrt(width // HEADS))
            if j == 2:
                projected = projected + r["qv_bias"][1:2, :]
            r["qkv"][j, rows, :] = projected.astype(BF)
            yield
        for pair in range(HEADS // 2):
            attention_forward(img, pair)
            yield
        if step is not None:
            wait_weights(step, range(3, 4))
        r["yb"][...] = (
            r["x"][rows, :].astype(F32)
            + dot(r["o"][rows, :], wg[unit_rows(OUT), :], 1, 0)
            + r["out_bias"][...]
        )
        yield
        norm_forward(img, lambda b, at: r["yb"][16 * b : 16 * (b + 1), :], 1, r["n2"], r["a2"])
        yield
        if step is not None:
            wait_weights(step, range(4, UNITS))
        result = None
        for j in range(4):
            hidden = dot(r["a2"][rows, :], wg[unit_rows(UP + j), :], 1, 0)
            hidden = hidden + r["up_bias"][:, width * j : width * (j + 1)]
            below = 0.5 + 0.5 * lax.erf(hidden * INV_SQRT2)
            slope = below + hidden * (jnp.exp(hidden * hidden * -0.5) * INV_SQRT2PI)
            active = (hidden * below).astype(BF)
            r["act"][j, rows, :] = active
            r["gp"][j, rows, :] = slope.astype(BF)
            term = dot(active, wg[unit_rows(DOWN_W + j), :], 1, 0)
            result = term if result is None else result + term
            yield
        yield r["yb"][...] + result + r["down_bias"][...]

    def keep_result(img, result):
        for at in range(0, seq, 16):
            write_bound(img, at, result[at : at + 16])

    def forward(step, img):
        @pl.when(first)
        def _():
            tail = image_rows(img, seq // 16 * 16, 16)
            r["x"][tail, :] = jnp.zeros((16, width), BF)
            own_copy("patches", img).wait()
            row = r["mask"][pl.ds(img, 1), :]
            at_row = lax.broadcasted_iota(jnp.int32, (pad, seq), 0)
            at_lane = lax.broadcasted_iota(jnp.int32, (pad, seq), 1)
            covered = jnp.where((at_row == at_lane) & (row == 1), 1.0, 0.0)
            column = jnp.sum(covered, axis=1, keepdims=True)
            r["cols"][image_rows(img), 2:3] = column
            token = r["token"][...][None, :].astype(F32)
            kept = r["pin"][img].astype(F32)
            mixed = jnp.where(column[:seq] > 0.5, token, kept)
            r["x"][image_rows(img, 0, seq), :] = mixed.astype(BF)

        @pl.when(second & (step == 0))
        def _():
            for at in range(images):
                own_copy("cotangent", at).wait()
                tail = at * pad + seq // 16 * 16
                r["dy"][tail : tail + 16, :] = jnp.zeros((16, width), BF)
                r["dy"][at * pad : at * pad + seq, :] = r["pin"][at]

        @pl.when(second)
        def _():
            forward_send(img).wait_recv()

        for result in forward_stages(img, step):
            pass

        @pl.when(step == 0)
        def _():
            pl.semaphore_wait(barrier, len(partners))

        @pl.when(first)
        def _():
            r["send"][image_rows(img), :] = result.astype(BF)
            forward_send(img).start()

        @pl.when(second)
        def _():
            keep_result(img, result)

    def norm_backward(img, which, gradient, incoming):
        results = []
        gain = r["gains"][which : which + 1, :]
        normed = r["n1"] if which == 0 else r["n2"]
        gain_sum = jnp.zeros((8, width), F32)
        shift_sum = jnp.zeros((8, width), F32)
        for b, rows in enumerate(row_blocks(img)):
            here = gradient[16 * b : 16 * (b + 1), :]
            unit = normed[rows, :].astype(F32)
            gain_sum = gain_sum + fold8(here * unit)
            shift_sum = shift_sum + fold8(here)
            scaled = here * gain
            mean = jnp.mean(scaled, axis=1, keepdims=True)
            along = jnp.mean(scaled * unit, axis=1, keepdims=True)
            local = (scaled - mean - unit * along) * r["cols"][rows, which : which + 1]
            results.append((b, rows, local + incoming(b, rows)))
        r["sm"][which : which + 1, :] += jnp.sum(gain_sum, axis=0, keepdims=True)
        r["sm"][2 + which : 3 + which, :] += jnp.sum(shift_sum, axis=0, keepdims=True)
        return results

    def backward_mlp_stages(img):
        rows = image_rows(img)
        incoming = r["dy"][rows, :]
        r["sm"][11:12, :] += jnp.sum(incoming.astype(F32), axis=0, keepdims=True)
        back = None
        for j in range(4):
            change = dot(incoming, wg[unit_rows(DOWN_W + j), :], 1, 1)
            change = change * r["gp"][j, rows, :].astype(F32)
            r["sm"][7 + j : 8 + j, :] += jnp.sum(change, axis=0, keepdims=True)
            narrow = change.astype(BF)
            r["gp"][j, rows, :] = narrow
            term = dot(narrow, wg[unit_rows(UP + j), :], 1, 1)
            back = term if back is None else back + term
            yield
        r["tb"][...] = back
        bias_sum = jnp.zeros((8, width), F32)
        for b, block_rows, middle in norm_backward(
            img, 1, r["tb"], lambda b, block_rows: r["dy"][block_rows, :].astype(F32)
        ):
            bias_sum = bias_sum + fold8(middle)
            r["da"][16 * b : 16 * (b + 1), :] = middle
            r["n2"][block_rows, :] = middle.astype(BF)
        r["sm"][6:7, :] += jnp.sum(bias_sum, axis=0, keepdims=True)
        yield

    def attention_backward_stages(img, pairs):
        rows = image_rows(img)
        places = [pl.ds(128 * pair, 128) for pair in pairs]
        loaded = []
        for pair, lanes in zip(pairs, places):
            probs = [r["prob"][img * HEADS + 2 * pair + head] for head in range(2)]
            loaded.append((*[r["qkv"][i, rows, lanes] for i in range(3)], r["do"][:, lanes], probs))
        results = []
        for queries, keys, values, back, probs in loaded:
            query_parts, key_parts, back_parts = halves(queries), halves(keys), halves(back)
            total = None
            for head in range(2):
                wide = probs[head].astype(F32)
                change = dot(values, back_parts[head], 1, 1)
                carried = jnp.sum(wide * change, axis=0, keepdims=True)
                scores = (wide * (change - carried)).astype(BF)
                terms = (
                    dot(scores, key_parts[head], 0, 0),
                    dot(scores, query_parts[head], 1, 0),
                    dot(probs[head], back_parts[head], 1, 0),
                )
                total = terms if total is None else [a + b for a, b in zip(total, terms)]
            d_query, d_key, d_value = total
            results.append((d_query * (1.0 / math.sqrt(width // HEADS)), d_key, d_value))
            yield
        for (d_query, d_key, d_value), lanes in zip(results, places):
            r["sm"][4:5, lanes] += jnp.sum(d_query, axis=0, keepdims=True)
            r["sm"][5:6, lanes] += jnp.sum(d_value, axis=0, keepdims=True)
            r["qkv"][0, rows, lanes] = d_query.astype(BF)
            r["qkv"][1, rows, lanes] = d_key.astype(BF)
            r["qkv"][2, rows, lanes] = d_value.astype(BF)

    def backward_attention_stages(img):
        rows = image_rows(img)
        r["do"][...] = dot(r["n2"][rows, :], wg[unit_rows(OUT), :], 1, 1).astype(BF)
        yield
        yield from attention_backward_stages(img, range(HEADS // 2))
        yield
        back = None
        for j in range(3):
            term = dot(r["qkv"][j, rows, :], wg[unit_rows(QKV + j), :], 1, 1)
            back = term if back is None else back + term
            yield
        r["tb"][...] = back
        for b, block_rows, entry in norm_backward(
            img, 0, r["tb"], lambda b, block_rows: r["da"][16 * b : 16 * (b + 1), :]
        ):
            r["da"][16 * b : 16 * (b + 1), :] = entry
        yield

    def send_back(img):
        r["send"][image_rows(img), :] = r["da"][...].astype(BF)
        backward_send(img).start()

    def run(stages):
        for _ in stages:
            pass

    def backward_attention(img):
        run(backward_attention_stages(img))

        @pl.when(first)
        def _():
            token_sum = jnp.zeros((8, width), F32)
            for b, block_rows in enumerate(row_blocks(img)):
                entry = r["da"][16 * b : 16 * (b + 1), :]
                under = r["cols"][block_rows, 2:3] > 0.5
                token_sum = token_sum + fold8(jnp.where(under, entry, 0.0))
                if 16 * b < seq:
                    write_bound(img, 16 * b, jnp.where(under, 0.0, entry))
            r["sm"][12:13, :] += jnp.sum(token_sum, axis=0, keepdims=True)

        @pl.when(second)
        def _():
            send_back(img)

    half_rows, quarter = width // 2, width // 4
    across_core, across_y = dp_at(1), dp_at(2)

    def core_copy(unit):
        return pltpu.make_async_remote_copy(
            src_ref=wg.at[unit_rows(unit, half_rows * (1 - core), half_rows), :],
            dst_ref=r["rc"].at[pl.ds(pl.multiple_of(unit * half_rows, 16), half_rows), :],
            send_sem=r["cs"].at[unit],
            recv_sem=r["cr"].at[unit],
            device_id=across_core,
        )

    in_order = UNITS - Z_FIRST

    def y_slot(unit, z_first):
        if z_first:
            at = in_order * quarter + unit // 4 * block
            return r["ry"].at[pl.ds(pl.multiple_of(at, 16), block), :]
        return r["ry"].at[pl.ds(pl.multiple_of(index_of(unit) * quarter, 16), quarter), :]

    def index_of(unit):
        return unit - 1 - jnp.minimum(unit // 4, Z_FIRST - 1)

    def unit_at(index):
        return index + 1 + jnp.minimum(index // 3, Z_FIRST - 1)

    def y_copy(unit, z_first, part=0):
        landing = y_slot(unit, z_first)
        if z_first:
            size, away = block, half_rows * core + 2 * block * z_at + block * (1 - y_at)
        else:
            size = 2 * block
            away = half_rows * core + quarter * (1 - y_at) + size * part
            landing = landing.at[pl.ds(size * part, size), :]
        return pltpu.make_async_remote_copy(
            src_ref=wg.at[unit_rows(unit, away, size), :],
            dst_ref=landing,
            send_sem=r["ys"].at[2 * unit + part],
            recv_sem=r["yr"].at[2 * unit + part],
            device_id=across_y,
        )

    def z_rows(unit, owner, z_first):
        if z_first:
            return unit_rows(unit, half_rows * core + 2 * block * owner, 2 * block)
        at = (0, 2, 3, 1)[owner]
        return unit_rows(unit, half_rows * core + quarter * y_at + block * at, block)

    def z_slot(unit, slot, z_first):
        if z_first:
            at = unit // 4 * 10 * block + slot * 2 * block
            return r["zf"].at[pl.ds(pl.multiple_of(at, 16), 2 * block), :]
        at = index_of(unit) * 5 * block + slot * block
        return r["zb"].at[pl.ds(pl.multiple_of(at, 16), block), :]

    def z_copy(unit, owner, toward, z_first, goes_to):
        up = toward > 0
        slot = owner if up or owner != goes_to else 4
        return pltpu.make_async_remote_copy(
            src_ref=wg.at[z_rows(unit, owner, z_first), :],
            dst_ref=z_slot(unit, slot, z_first),
            send_sem=r["rs" if up else "ls"].at[unit * 4 + owner],
            recv_sem=r["rr" if up else "lr"].at[unit * 4 + owner],
            device_id={"dp": lax.rem(me + n + 4 * toward, n), "section": sec},
        )

    def add_rows(unit, offset, source, size):
        for part in range(size // block):
            rows = unit_rows(unit, offset + block * part, block)
            came = source[block * part : block * (part + 1), :]
            wg[rows, :] = (wg[rows, :].astype(F32) + came.astype(F32)).astype(BF)

    def add_core(unit, z_first):
        core_copy(unit).wait_recv()
        came = r["rc"].at[pl.ds(pl.multiple_of(unit * half_rows, 16), half_rows), :]
        add_rows(unit, half_rows * core, came, half_rows)
        if z_first:
            z_start(unit, True)
        else:
            for part in range(2):
                y_copy(unit, False, part).start()

    def z_start(unit, z_first, from_bottom=(3, 2, 1), from_top=(0, 1, 2)):
        @pl.when(z_at == 0)
        def _():
            for owner in from_bottom:
                z_copy(unit, owner, 1, z_first, 1).start()

        @pl.when(z_at == 3)
        def _():
            for owner in from_top:
                z_copy(unit, owner, -1, z_first, 2).start()

    def z_hop(hop, unit, z_first):
        size = 2 * block if z_first else block

        def pass_on(here, owner, toward):
            z_copy(unit, owner, toward, z_first, here).wait_recv()
            rows = z_rows(unit, owner, z_first)
            came = z_slot(unit, owner, z_first)
            wg[rows, :] = (wg[rows, :].astype(F32) + came[...].astype(F32)).astype(BF)
            z_copy(unit, owner, toward, z_first, here + toward).start()

        def finish(here):
            total = wg[z_rows(unit, here, z_first), :].astype(F32)
            if here > 0:
                z_copy(unit, here, 1, z_first, here).wait_recv()
                total = total + z_slot(unit, here, z_first)[...].astype(F32)
            if here < 3:
                z_copy(unit, here, -1, z_first, here).wait_recv()
                total = total + z_slot(unit, 4, z_first)[...].astype(F32)
            if z_first:
                wg[z_rows(unit, here, True), :] = total.astype(BF)
            else:
                put(unit, total)

        @pl.when(z_at == hop)
        def _():
            for owner in range(3, hop, -1):
                pass_on(hop, owner, 1)
            if hop >= 2:
                finish(hop)

        @pl.when(z_at == 3 - hop)
        def _():
            for owner in range(3 - hop):
                pass_on(3 - hop, owner, -1)
            if hop >= 2:
                finish(3 - hop)

    def put_copy(unit):
        return pltpu.make_async_copy(r["stage"].at[unit], r["grads"].at[unit], r["put_sem"].at[unit])

    def put(unit, total):
        r["stage"][unit] = total * scale
        put_copy(unit).start()

    def finish_z_first(unit):
        y_copy(unit, True).wait_recv()
        mine = unit_rows(unit, half_rows * core + 2 * block * z_at + block * y_at, block)
        came = y_slot(unit, True)[...]
        put(unit, wg[mine, :].astype(F32) + came.astype(F32))

    def add_y(unit):
        size = 2 * block
        for part in range(2):
            y_copy(unit, False, part).wait_recv()
            came = y_slot(unit, False).at[pl.ds(size * part, size), :]
            add_rows(unit, half_rows * core + quarter * y_at + size * part, came, size)
            if part == 0:
                z_start(unit, False, (3,), (0,))
            else:
                z_start(unit, False, (2, 1), (1, 2))

    def place(owner, z_first):
        core_of, y_of, z_of = lax.rem(owner, 2), lax.rem(owner // 2, 2), owner // 4
        if z_first:
            return core_of * 8 + z_of * 2 + y_of
        return core_of * 8 + y_of * 4 + jnp.where(z_of == 0, 0, jnp.where(z_of == 3, 1, z_of + 1))

    def weight_gradient(left, right, chunk, first_unit, spread, z_first=False):
        for half in range(2):
            product = dot(left(half), right, 0, 0).astype(BF)
            for b in range(8):
                at = chunk * 16 + 8 * half + b
                if spread == 1:
                    at = 8 * half + b
                if reduce_here:
                    owner, part = at // spread, lax.rem(at, spread)
                    if spread == 4:
                        part = b % spread
                        z_first = part == 0
                    rows = unit_rows(first_unit + part, place(owner, z_first) * block, block)
                else:
                    rows = unit_rows(first_unit, at * block, block)
                wg[rows, :] = product[block * b : block * (b + 1), :]

    def half_lanes(half):
        return pl.ds((width // 2) * half, width // 2)

    def down_gradient():
        def one(z_first):
            def body(j, carry):
                weight_gradient(
                    lambda half: r["dy"][:, half_lanes(half)], r["act"][j], j, j, 1, z_first
                )
                if reduce_here:
                    core_copy(j).start()
                    if not z_first:
                        pl.when(j == 1)(lambda: add_core(0, True))
                        pl.when(j > 1)(lambda: add_core(j - 1, False))
                return carry

            return body

        lax.fori_loop(0, 1, one(True), 0)
        lax.fori_loop(1, 4, one(False), 0)
        if reduce_here:
            add_core(3, False)

    def start_units(begin, end):
        if reduce_here:
            for unit in range(begin, end):
                core_copy(unit).start()

    def add_y_if(when, unit):
        if reduce_here:
            pl.when(when)(lambda: add_y(unit))

    def turn(step, carry):
        img = lax.rem(step, images)
        early = step < images
        back_now = early == second
        down_now = step == jnp.where(first, 2 * images - 1, images)

        @pl.when(early)
        def _():
            forward(step, img)

        @pl.when(back_now & first)
        def _():
            backward_send(img).wait_recv()

        @pl.when(down_now)
        def _():
            down_gradient()

        @pl.when(back_now)
        def _():
            run(backward_mlp_stages(img))

        @pl.when(back_now)
        def _():
            backward_attention(img)

        return carry

    lax.fori_loop(0, 2 * images, turn, 0)

    def up_one(c, carry):
        weight_gradient(lambda half: r["gp"][c, :, half_lanes(half)], r["a2"][...], c, UP, 4)
        return carry

    add_y_if(first, 1)
    lax.fori_loop(0, 4, up_one, 0)
    start_units(UP, OUT)
    if reduce_here:
        add_core(UP, True)
        for unit in range(UP + 1, OUT):
            add_core(unit, False)
    add_y_if(first, 2)
    add_y_if(second, 1)
    weight_gradient(lambda half: r["n2"][:, half_lanes(half)], r["o"][...], 0, OUT, 1, Z_FIRST == 3)
    start_units(OUT, QKV)

    def qkv_one(c, carry):
        weight_gradient(lambda half: r["qkv"][c, :, half_lanes(half)], r["a1"][...], c, QKV, 3)
        return carry

    lax.fori_loop(0, 3, qkv_one, 0)
    start_units(QKV, UNITS)
    if reduce_here and Z_FIRST == 3:
        add_core(OUT, True)

    for img in range(images):
        bound_copy(img).start()

    def finish_images():
        for img in range(images):
            bound_copy(img).wait()

            @pl.when(first)
            def _(img=img):
                forward_send(img).wait_send()

            @pl.when(second)
            def _(img=img):
                backward_send(img).wait_send()

    if reduce_here:
        hops = [dp_at(1), dp_at(2), dp_at(8), dp_at(4), across]

        def small_send(t):
            return pltpu.make_async_remote_copy(
                src_ref=r["sms"].at[t],
                dst_ref=r["smr"].at[t],
                send_sem=r["ss"].at[t],
                recv_sem=r["sr"].at[t],
                device_id=hops[t],
            )

        r["sms"][0] = r["sm"][...]
        small_send(0).start()

        def small_step(t):
            small_send(t).wait_recv()
            if t < 4:
                r["sms"][t + 1] = r["sms"][t] + r["smr"][t]
                small_send(t + 1).start()
                return
            total = r["sms"][4] * scale
            shift = lax.rem(width - block * me, width)
            r["small"][...] = pltpu.roll(total, shift, 1)
            r["small"][12:13, :] = (r["sms"][4, 12:13, :] + r["smr"][4, 12:13, :]) * scale
            up_row = r["sms"][4, pl.ds(7 + me // 4, 1), :] * scale
            up_shift = lax.rem(width - 4 * block * lax.rem(me, 4), width)
            spread_row = jnp.broadcast_to(up_row, (8, width))
            r["small"][13:14, :] = pltpu.roll(spread_row, up_shift, 1)[0:1]

        def sent(unit, z_first):
            core_copy(unit).wait_send()
            for part in range(1 if z_first else 2):
                y_copy(unit, z_first, part).wait_send()
            for here in range(4):

                @pl.when(z_at == here)
                def _(here=here):
                    for owner in range(4):
                        if owner > here:
                            z_copy(unit, owner, 1, z_first, here + 1).wait_send()
                        if owner < here:
                            z_copy(unit, owner, -1, z_first, here - 1).wait_send()

            put_copy(unit).wait()

        def drain(k, carry):
            @pl.when((k < in_order) & ((k > 1) | second))
            def _():
                add_y(unit_at(k))

            @pl.when((k > 1) & (k + WINDOW < in_order))
            def _():
                add_core(unit_at(k + WINDOW), False)

            for hop in (1, 2, 3):

                @pl.when((k >= LAG[hop]) & (k < LAG[hop] + Z_FIRST))
                def _(hop=hop):
                    z_hop(hop, 4 * (k - LAG[hop]), True)

            for hop in (1, 2, 3):

                @pl.when((k >= LAG[hop]) & (k < in_order + LAG[hop]))
                def _(hop=hop):
                    z_hop(hop, unit_at(k - LAG[hop]), False)

            for t in range(5):

                @pl.when(k == SMALL_AT[t])
                def _(t=t):
                    small_step(t)

            @pl.when((k >= LAG[3] + 1) & (k < LAG[3] + 1 + Z_FIRST))
            def _():
                y_copy(4 * (k - LAG[3] - 1), True).start()

            @pl.when((k >= in_order) & (k < in_order + Z_FIRST))
            def _():
                finish_z_first(4 * (k - in_order))

            @pl.when(k == 3)
            def _():
                finish_images()

            @pl.when(k >= LAG[3] + 2)
            def _():
                sent(unit_at(k - LAG[3] - 2), False)

            return carry

        lax.fori_loop(1, in_order + LAG[3], drain, 0)

        for unit in range(0, 4 * Z_FIRST, 4):
            sent(unit, True)
        for index in range(in_order - 2, in_order):
            sent(unit_at(index), False)
        for t in range(5):
            small_send(t).wait_send()
    else:
        r["small"][...] = r["sm"][...] * scale
        out = pltpu.make_async_copy(wg.at[pl.ds(0, UNITS * width), :], r["grads"], r["pin_sem"].at[0])
        out.start()
        out.wait()
        finish_images()


def hand_on(bound, grads, small, *refs):
    out_bound, down, up, out, three = refs[:5]
    vectors = refs[5:12]
    held_bound, held_grads, held_small = refs[12:15]
    held_vectors = refs[15:22]
    load_sem, store_sem, small_sem, vector_sem = refs[22:]
    images = bound.shape[0]
    units, block, width = grads.shape

    def target(unit):
        if unit < UP:
            return down.at[:, pl.ds(width * unit, width)]
        if unit < OUT:
            return up.at[pl.ds(block * (unit - UP), block), :]
        if unit < QKV:
            return out
        return three.at[pl.ds(block * (unit - QKV), block), :]

    moves = [(bound.at[i], held_bound.at[i], out_bound.at[i]) for i in range(images)]
    moves += [(grads.at[unit], held_grads.at[unit], target(unit)) for unit in range(units)]
    loads = [
        pltpu.make_async_copy(source, held, load_sem.at[i])
        for i, (source, held, _) in enumerate(moves)
    ]
    stores = [
        pltpu.make_async_copy(held, result, store_sem.at[i])
        for i, (_, held, result) in enumerate(moves)
    ]
    load_small = pltpu.make_async_copy(small, held_small, small_sem)
    vector_stores = [
        pltpu.make_async_copy(held, result, vector_sem.at[i])
        for i, (held, result) in enumerate(zip(held_vectors, vectors))
    ]
    load_small.start()
    for load in loads:
        load.start()
    load_small.wait()
    gains, shifts, qv, out_vector, up_vector, down_vector, token = held_vectors
    gains[0] = held_small[0:2, :block]
    shifts[0] = held_small[2:4, :block]
    qv[0] = held_small[4:6, :block]
    out_vector[...] = held_small[6:7, :block]
    down_vector[...] = held_small[11:12, :block]
    up_vector[...] = held_small[13:14, : 4 * block]
    token[...] = held_small[12:13, :].reshape(width)
    for store in vector_stores:
        store.start()
    for load, store in zip(loads, stores):
        load.wait()
        store.start()
    for store in stores + vector_stores:
        store.wait()


def on_device(n, *args):
    (patches, block_mask, mask_token, norm_gains, norm_shifts, w_qkv, qv_bias, w_out, out_bias) = args[:9]
    w_up, up_bias, w_down, down_bias, cotangent = args[9:]
    images, seq, width = patches.shape
    pad = -(-seq // 16) * 16
    rows = images * pad
    reduce_here = n == 16
    scale = 1.0 / math.sqrt(images * n * seq)
    geo = (n, images, seq, pad, width, scale)
    block = width // 16
    anywhere = pl.BlockSpec(memory_space=pl.ANY)
    vmem = pl.BlockSpec(memory_space=pltpu.VMEM)
    bound_shape = jax.ShapeDtypeStruct((images, seq, 1, width), F32)
    if reduce_here:
        grads_shape = jax.ShapeDtypeStruct((UNITS, block, width), F32)
    else:
        grads_shape = jax.ShapeDtypeStruct((UNITS * width, width), BF)
    out_shape = [bound_shape, grads_shape, jax.ShapeDtypeStruct((SMALL, width), F32)]
    narrow = pltpu.VMEM((rows, width), BF)
    dma = pltpu.SemaphoreType.DMA
    scratch = [
        pltpu.VMEM((16 * width, width), BF),
        narrow,
        narrow,
        narrow,
        pltpu.VMEM((3, rows, width), BF),
        narrow,
        narrow,
        narrow,
        pltpu.VMEM((4, rows, width), BF),
        pltpu.VMEM((4, rows, width), BF),
        narrow,
        narrow,
        pltpu.VMEM((images * HEADS, pad, pad), BF),
        pltpu.VMEM((rows, 3), F32),
        pltpu.VMEM((pad, width), F32),
        pltpu.VMEM((pad, width), F32),
        pltpu.VMEM((pad, width), F32),
        pltpu.VMEM((pad, width), BF),
        pltpu.VMEM((images, seq, width), BF),
        pltpu.VMEM((images, seq, 1, width), F32),
        pltpu.VMEM((SMALL, width), F32),
        pltpu.VMEM((5, SMALL, width), F32),
        pltpu.VMEM((5, SMALL, width), F32),
        dma((images,)),
        dma((UNITS,)),
        dma((images,)),
        dma((images,)),
        dma((images,)),
        dma((images,)),
        dma((images,)),
    ]
    if reduce_here:
        scratch += [
            pltpu.VMEM((UNITS, block, width), F32),
            pltpu.VMEM((UNITS * width // 2, width), BF),
            pltpu.VMEM((((UNITS - Z_FIRST) * 4 + Z_FIRST) * block, width), BF),
            pltpu.VMEM(((UNITS - Z_FIRST) * 5 * block, width), BF),
            pltpu.VMEM((Z_FIRST * 10 * block, width), BF),
        ]
        scratch += [dma((UNITS,))] * 2 + [dma((UNITS * 2,))] * 2 + [dma((UNITS * 4,))] * 4 + [dma((5,))] * 2 + [dma((UNITS,))]
    weights = 12 * width * width
    bound, grads, small = pl.pallas_call(
        functools.partial(kernel, geo),
        out_shape=out_shape,
        in_specs=[anywhere] * 2 + [vmem] * 8 + [anywhere] * 4,
        out_specs=[anywhere, anywhere, vmem],
        scratch_shapes=scratch,
        compiler_params=pltpu.CompilerParams(
            collective_id=0, has_side_effects=True, vmem_limit_bytes=64 * 1024 * 1024 - 65536
        ),
        cost_estimate=pl.CostEstimate(
            flops=6 * rows * weights, bytes_accessed=4 * weights, transcendentals=rows * width * 8
        ),
        name="relay",
    )(
        patches,
        cotangent,
        block_mask,
        mask_token,
        norm_gains[0],
        norm_shifts[0],
        qv_bias[0],
        out_bias,
        up_bias,
        down_bias,
        w_qkv,
        w_out,
        w_up,
        w_down,
    )
    if reduce_here:
        shapes = [(block, 4 * width), (4 * block, width), (block, width), (3 * block, width)]
        shapes += [(1, 2, block)] * 3 + [(1, block), (1, 4 * block), (1, block), (width,)]
        results = pl.pallas_call(
            hand_on,
            out_shape=[bound_shape] + [jax.ShapeDtypeStruct(shape, F32) for shape in shapes],
            in_specs=[anywhere] * 3,
            out_specs=[anywhere] * 12,
            scratch_shapes=[
                pltpu.VMEM(bound_shape.shape, F32),
                pltpu.VMEM(grads_shape.shape, F32),
                pltpu.VMEM((SMALL, width), F32),
                *[pltpu.VMEM(shape, F32) for shape in shapes[4:]],
                dma((images + UNITS,)),
                dma((images + UNITS,)),
                dma(()),
                dma((len(shapes) - 4,)),
            ],
            name="hand_on",
        )(bound, grads, small)
        bound, down, up, out, qkv, gains, shifts, qv, out_vector, up_vector, down_vector, token = results
        boundary = bound.transpose(2, 0, 1, 3)
        parts = (boundary, token, gains, shifts, qkv.T[None], qv, out.T[None], out_vector, up.T[None])
        return (*parts, up_vector, down.T[None], down_vector)
    me = lax.axis_index("dp")
    share = width // n
    token = lax.psum(small[12], ("dp", "section"))
    vectors = lax.psum(small[:12], "dp")
    wide = grads.astype(F32) * scale

    def scattered(first, count):
        part = wide[first * width : (first + count) * width]
        return lax.psum_scatter(part, "dp", scatter_dimension=0, tiled=True).T

    down = lax.psum_scatter(
        wide[: 4 * width].reshape(4, width, width), "dp", scatter_dimension=1, tiled=True
    )
    down = down.transpose(0, 2, 1).reshape(4 * width, share)
    up = scattered(UP, 4)
    out = scattered(OUT, 1)
    qkv = scattered(QKV, 3)

    def cut(first, count):
        return lax.dynamic_slice(vectors, (first, me * share), (count, share))

    up_vector = lax.dynamic_slice(vectors[7:11].reshape(-1), (me * 4 * share,), (4 * share,))
    parts = (bound.transpose(2, 0, 1, 3), token, cut(0, 2)[None], cut(2, 2)[None], qkv[None])
    parts += (cut(4, 2)[None], out[None], cut(6, 1), up[None], up_vector[None], down[None], cut(11, 1))
    return parts


def solution(mesh):
    return jax.shard_map(
        functools.partial(on_device, mesh.shape["dp"]),
        mesh=mesh,
        in_specs=(
            P("dp", None, None),
            P("dp", None),
            P(),
            P("section", None, None),
            P("section", None, None),
            P("section", None, None),
            P("section", None, None),
            P("section", None, None),
            P("section", None),
            P("section", None, None),
            P("section", None),
            P("section", None, None),
            P("section", None),
            P("dp", None, None),
        ),
        out_specs=(
            P("section", "dp", None, None),
            P(),
            P("section", None, "dp"),
            P("section", None, "dp"),
            P("section", None, "dp"),
            P("section", None, "dp"),
            P("section", None, "dp"),
            P("section", "dp"),
            P("section", None, "dp"),
            P("section", "dp"),
            P("section", None, "dp"),
            P("section", "dp"),
        ),
        check_vma=False,
    )
```
